32 devices in a mesh: sta: 4 (over y, x), evt: 8 (over z, core).
Axes of the slice: x: 2, y: 2, z: 4, core: 2. Of those that a mesh axis runs over, the one named last changes fastest.
Arguments:
- traces: bfloat16 [3, 32, 512, 2048], P(None, 'sta', 'evt'), may hold values from -96 to 96
- baz_bin: int32 [32, 512], P('sta', 'evt'), may hold values from 0 to 35
- inc_bin: int32 [32, 512], P('sta', 'evt'), may hold values from 0 to 7
- counts: int32 [32], P('sta'), may hold values from 64 to 512
- depth_index: int32 [32, 512], P('sta'), may hold values from 0 to 2046
- tile_of: int32 [32], replicated, may hold values from 0 to 15
Outputs:
- stack: float32 [16, 5, 2, 512], P('sta', None, None, 'evt')
The draws below stay inside these ranges and needn't reach their ends.
All inputs are finite; a program needn't handle non-finite values.
Results may differ from the reference program's by a relative error of at most 0.0003.
Values sent between devices are 32-bit elements; how exact they have to be, the bound alone decides.
A program may use at most 64 MiB of HBM per device.

```python
import jax
import jax.numpy as jnp
from jax import lax

NS = 2048
DEPTHS = 512
BAZ_BINS = 36
INC_BINS = 8
STATIONS = 32
EVENTS = 512
TILES = 16


def set_ends(result, own_key, low, top_value):
    longest = result.shape.index(max(result.shape))
    spots = []
    for shift in (0, 1):
        where = [jax.random.randint(jax.random.fold_in(own_key, axis), (), 0, length) for axis, length in enumerate(result.shape)]
        where[longest] = (where[longest] + shift) % result.shape[longest]
        spots.append(tuple(where))
    return result.at[spots[0]].set(low).at[spots[1]].set(top_value)


def block_scale(stream_key, dims, shards, low, high):
    factor_of = 1.0
    for dim, parts in shards:
        steps = jax.random.uniform(jax.random.fold_in(jax.random.fold_in(stream_key, 6), dim), (parts,), jnp.float32, low / len(shards), high / len(shards))
        factor_of = factor_of * jnp.repeat(jnp.exp(steps), dims[dim] // parts).reshape((-1,) + (1,) * (len(dims) - 1 - dim))
    return factor_of


def centred(own_key, shape, deviation, bound, shards=(), kind=jnp.bfloat16):
    result = deviation * jax.random.normal(own_key, shape, jnp.float32)
    if shards:
        result = result * block_scale(own_key, shape, shards, -0.22, 0.18)
    return jnp.clip(result, -bound, bound).astype(kind)


def setup_inputs(seed: int = 0) -> dict:
    key_of = jax.random.split(jax.random.key(seed), 7)
    return {
        "traces": centred(key_of[0], (3, STATIONS, EVENTS, NS), 16.0, 96.0, ((1, 4), (2, 8))),
        "baz_bin": set_ends(jax.random.randint(key_of[1], (STATIONS, EVENTS), 0, BAZ_BINS), jax.random.fold_in(key_of[1], 1), 0, BAZ_BINS - 1).astype(jnp.int32),
        "inc_bin": set_ends(jax.random.randint(key_of[2], (STATIONS, EVENTS), 0, INC_BINS), jax.random.fold_in(key_of[2], 1), 0, INC_BINS - 1).astype(jnp.int32),
        "counts": set_ends(jax.random.randint(key_of[3], (STATIONS,), EVENTS // 8, EVENTS + 1), jax.random.fold_in(key_of[3], 1), EVENTS // 8, EVENTS).astype(jnp.int32),
        "depth_index": set_ends(jax.random.randint(key_of[4], (STATIONS, DEPTHS), 0, NS - 1), jax.random.fold_in(key_of[4], 1), 0, (NS - 1) - 1).astype(jnp.int32),
        "tile_of": set_ends(jax.random.randint(key_of[5], (STATIONS,), 0, TILES), jax.random.fold_in(key_of[5], 1), 0, TILES - 1).astype(jnp.int32),
    }


def reference(traces, baz_bin, inc_bin, counts, depth_index, tile_of):
    highest = lax.Precision.HIGHEST

    def one_station(station):
        block = lax.dynamic_index_in_dim(traces, station, 1, keepdims=False).astype(jnp.float32)
        bins = lax.dynamic_index_in_dim(baz_bin, station, 0, keepdims=False)
        tilts = lax.dynamic_index_in_dim(inc_bin, station, 0, keepdims=False)
        total = lax.dynamic_index_in_dim(counts, station, 0, keepdims=False)
        indices = lax.dynamic_index_in_dim(depth_index, station, 0, keepdims=False).astype(jnp.int32)
        phi = (bins.astype(jnp.float32) + 0.5) * (2.0 * jnp.pi / BAZ_BINS)
        incidence = (12.0 + 2.5 * (tilts.astype(jnp.float32) + 0.5)) * (jnp.pi / 180.0)
        cosine = jnp.cos(phi)[:, None]
        sine = jnp.sin(phi)[:, None]
        radial = -(cosine * block[1] + sine * block[2])
        quality = jnp.cos(incidence)[:, None] * radial + jnp.sin(incidence)[:, None] * block[0]
        transverse = sine * block[1] - cosine * block[2]
        data = jnp.concatenate([quality, transverse], axis=1)
        live = (jnp.arange(EVENTS) < total).astype(jnp.float32)
        harm = jnp.stack([jnp.ones_like(phi), jnp.cos(phi), jnp.sin(phi), jnp.cos(2.0 * phi), jnp.sin(2.0 * phi)], axis=1)
        weighted = harm * live[:, None]
        normal = jnp.dot(weighted.T, harm, precision=highest) + jnp.eye(5, dtype=jnp.float32)
        rhs = jnp.dot(weighted.T, data, precision=highest)
        coeff = jnp.linalg.solve(normal, rhs).reshape(5, 2, NS)
        return 0.5 * (coeff[:, :, indices] + coeff[:, :, indices + 1])
    profiles = lax.map(one_station, jnp.arange(STATIONS))
    onehot = (tile_of[None, :] == jnp.arange(TILES)[:, None]).astype(jnp.float32)
    sums = jnp.einsum('ts,skcz->tkcz', onehot, profiles, precision=highest)
    members = jnp.sum(onehot, axis=1)
    return sums / jnp.maximum(members, 1.0)[:, None, None, None]
```

```python
import functools

import jax
import jax.numpy as jnp
from jax import lax
from jax.experimental import pallas as pl
from jax.experimental.pallas import tpu as pltpu
from jax.sharding import PartitionSpec as P

BAZ_BINS = 36
HARMS = 5
LANES = 128
ROWS = 8
TERMS = 16
HALF = LANES // 2
GROUPS = (4, 4)
SPLITS = 3
MESH = pl.DeviceIdType.MESH


def pick_lanes(values, lanes):
    return jnp.take_along_axis(values, lanes, axis=1, mode="promise_in_bounds")


def groups_of(stations):
    groups, at = [], 0
    while at < stations:
        size = min(GROUPS[len(groups)] if len(groups) < len(GROUPS) else 1, stations - at)
        groups.append(range(at, at + size))
        at += size
    return groups


def kernel(
    evt_count,
    sta_count,
    tiles,
    traces_ref,
    baz_hbm,
    inc_hbm,
    counts_hbm,
    depth_hbm,
    tile_hbm,
    out_ref,
    trace_buf,
    baz_ref,
    inc_ref,
    counts_ref,
    depth_ref,
    tile_ref,
    weight_buf,
    left_buf,
    normal_buf,
    normal_recv,
    split_buf,
    hot_buf,
    part_buf,
    part_pair,
    tile_buf,
    tile_recv,
    load_sem,
    small_sem,
    pair_sem,
    normal_send_sem,
    normal_recv_sem,
    tile_send_sem,
    tile_recv_sem,
):
    stations, slots = baz_ref.shape
    samples = traces_ref.shape[3]
    depths = depth_ref.shape[1]
    share = depths // evt_count
    used = HARMS * stations
    evt = lax.axis_index("evt")
    sta = lax.axis_index("sta")
    chips = evt_count // 2
    core = evt % 2
    chip = evt // 2
    partner = {"evt": evt + 1 - 2 * core}
    f32 = jnp.float32

    def load(s):
        return pltpu.make_async_copy(traces_ref.at[:, s], trace_buf.at[s], load_sem.at[s])

    def peers(act):
        def one(n, carry):
            to_chip, to_sta = n // sta_count, n % sta_count

            @pl.when(jnp.logical_or(to_chip != chip, to_sta != sta))
            def _():
                act(to_sta, to_chip)

            return carry

        lax.fori_loop(0, chips * sta_count, one, 0, unroll=chips * sta_count <= 16)

    barrier = pltpu.get_barrier_semaphore()
    for j in range(1, evt_count):
        pl.semaphore_signal(
            barrier, inc=1, device_id={"evt": lax.rem(evt + j, evt_count)},
            device_id_type=MESH,
        )

    def greet(to_sta, to_chip):
        @pl.when(to_sta != sta)
        def _():
            pl.semaphore_signal(
                barrier, inc=1, device_id={"sta": to_sta, "evt": 2 * to_chip + core},
                device_id_type=MESH,
            )

    peers(greet)
    small = [
        pltpu.make_async_copy(src, dst, small_sem.at[n])
        for n, (src, dst) in enumerate(
            [
                (baz_hbm, baz_ref),
                (inc_hbm, inc_ref),
                (counts_hbm, counts_ref),
                (depth_hbm, depth_ref),
                (tile_hbm, tile_ref),
            ]
        )
    ]
    for copy in small:
        copy.start()
    for s in range(stations):
        load(s).start()

    for copy in small:
        copy.wait()

    phi = (baz_ref[...].astype(f32) + 0.5) * (2.0 * jnp.pi / BAZ_BINS)
    tilt = (12.0 + 2.5 * (inc_ref[...].astype(f32) + 0.5)) * (jnp.pi / 180.0)
    cosine, sine = jnp.cos(phi), jnp.sin(phi)
    cos_tilt, sin_tilt = jnp.cos(tilt), jnp.sin(tilt)
    row_ids = lax.broadcasted_iota(jnp.int32, (stations, slots), 0)
    total = jnp.zeros((stations, slots), jnp.int32)
    for s in range(stations):
        total = jnp.where(row_ids == s, counts_ref[s], total)
    slot_ids = evt * slots + lax.broadcasted_iota(jnp.int32, (stations, slots), 1)
    live = jnp.where(slot_ids < total, 1.0, 0.0).astype(f32)
    harm = [
        jnp.ones_like(phi),
        cosine,
        sine,
        2.0 * cosine * cosine - 1.0,
        2.0 * sine * cosine,
    ]
    weighted = [h * live for h in harm]
    parts = [
        [sin_tilt, -cos_tilt * cosine, -cos_tilt * sine],
        [jnp.zeros_like(phi), sine, -cosine],
    ]
    weight_buf[...] = jnp.zeros_like(weight_buf)
    for c in range(2):
        for k in range(HARMS):
            at = (c * ROWS + k) * stations
            for m in range(3):
                lane = m * slots
                weight_buf[
                    lane // LANES, at:at + stations, lane % LANES:lane % LANES + slots
                ] = weighted[k] * parts[c][m]
    for s in range(stations):
        for n in range(weight_buf.shape[0]):
            weights = weight_buf[n, pl.ds(s, 2 * ROWS, stride=stations), :]
            high = weights.astype(jnp.bfloat16)
            low = (weights - high.astype(f32)).astype(jnp.bfloat16)
            left_buf[s, 0:2 * ROWS, n * LANES:(n + 1) * LANES] = high
            left_buf[s, 2 * ROWS:4 * ROWS, n * LANES:(n + 1) * LANES] = low
    lane_ids = lax.broadcasted_iota(jnp.int32, (stations, LANES), 1)
    station_ids = lax.broadcasted_iota(jnp.int32, (stations, LANES), 0)
    packed = jnp.zeros((stations, LANES), f32)
    place = 0
    for k in range(HARMS):
        for l in range(k + 1):
            column = jnp.sum(weighted[k] * harm[l], axis=1, keepdims=True)
            packed = jnp.where(lane_ids % TERMS == place, column, packed)
            place += 1
    packed = jnp.where(lane_ids // TERMS == station_ids, packed, 0.0)
    normal_buf[0:1] = jnp.sum(packed, axis=0, keepdims=True)

    def normals(j):
        return pltpu.make_async_remote_copy(
            src_ref=normal_buf.at[0:1],
            dst_ref=normal_recv.at[j - 1, 0:1],
            send_sem=normal_send_sem.at[j - 1],
            recv_sem=normal_recv_sem.at[j - 1],
            device_id={"evt": lax.rem(evt + j, evt_count)},
            device_id_type=MESH,
        )

    part_swap = pltpu.make_async_remote_copy(
        src_ref=part_buf.at[1 - core, :, 0:used],
        dst_ref=part_pair,
        send_sem=pair_sem.at[0],
        recv_sem=pair_sem.at[1],
        device_id=partner,
        device_id_type=MESH,
    )

    def sums(to_sta, to_chip):
        return pltpu.make_async_remote_copy(
            src_ref=tile_buf.at[to_chip, to_sta],
            dst_ref=tile_recv.at[chip, sta],
            send_sem=tile_send_sem.at[to_chip, to_sta],
            recv_sem=tile_recv_sem.at[chip, sta],
            device_id={"sta": to_sta, "evt": 2 * to_chip + core},
            device_id_type=MESH,
        )

    def sums_from(from_sta, from_chip):
        return pltpu.make_async_remote_copy(
            src_ref=tile_buf.at[from_chip, from_sta],
            dst_ref=tile_recv.at[from_chip, from_sta],
            send_sem=tile_send_sem.at[from_chip, from_sta],
            recv_sem=tile_recv_sem.at[from_chip, from_sta],
            device_id={"sta": from_sta, "evt": 2 * from_chip + core},
            device_id_type=MESH,
        )

    late = 2 * chip >= chips

    def open_up():
        pl.semaphore_wait(barrier, evt_count - 1 + (sta_count - 1) * chips)
        for j in range(1, evt_count):
            normals(j).start()

    pl.when(late)(open_up)

    lane8 = lax.broadcasted_iota(jnp.int32, (ROWS, LANES), 1)

    parts_of = samples // LANES
    window_ids = lax.broadcasted_iota(jnp.int32, (LANES, depths), 0)

    def right_sides(s):
        block = trace_buf[s].reshape(3 * slots, samples)
        right = jnp.dot(left_buf[s, :, 0:3 * slots], block, preferred_element_type=f32)
        pair = right[0:2 * ROWS] + right[2 * ROWS:4 * ROWS]
        pair = pair + pltpu.roll(pair, samples - 1, 1)
        high = pair.astype(jnp.bfloat16)
        low = (pair - high.astype(f32)).astype(jnp.bfloat16)
        lane = lax.bitwise_and(depth_ref[s:s + 1, :], LANES - 1)
        hot = jnp.where(window_ids == lane, 0.5, 0.0).astype(jnp.bfloat16)
        hot_buf[s] = hot
        for n in range(parts_of):
            at = n * LANES
            split_buf[s, n * 2 * ROWS:(n + 1) * 2 * ROWS, 0:LANES] = high[:, at:at + LANES]
            split_buf[s, n * 2 * ROWS:(n + 1) * 2 * ROWS, LANES:] = low[:, at:at + LANES]

    def pick(s):
        hot = hot_buf[s]
        found = jnp.dot(
            split_buf[s], jnp.concatenate([hot, hot], axis=0), preferred_element_type=f32
        )
        chunk = lax.shift_right_logical(depth_ref[s:s + 1, :], 7)
        chunk = jnp.broadcast_to(chunk, (2 * ROWS, depths))
        got = found[0:2 * ROWS]
        for n in range(1, parts_of):
            got = jnp.where(chunk == n, found[n * 2 * ROWS:(n + 1) * 2 * ROWS], got)
        for z in range(depths // LANES):
            first = got[0:ROWS, z * LANES:(z + 1) * LANES]
            second = got[ROWS:2 * ROWS, z * LANES:(z + 1) * LANES]
            for d in range(LANES // share):
                left = first if d == 0 else pltpu.roll(first, LANES - d * share, 1)
                move = (HALF - d * share) % LANES
                rest = second if move == 0 else pltpu.roll(second, move, 1)
                to = z * (LANES // share) + d
                part_buf[to % 2, to // 2, pl.ds(s, ROWS, stride=stations), :] = jnp.where(
                    lane8 < HALF, left, rest
                )

    groups = groups_of(stations)
    for g, group in enumerate(groups):
        for s in group:
            load(s).wait()
        if g == len(groups) - 1:
            pl.when(jnp.logical_not(late))(open_up)
        for s in group:
            right_sides(s)
        if g > 0:
            for s in groups[g - 1]:
                pick(s)
    for s in groups[-1]:
        pick(s)
    part_swap.start()

    block = tile_rows(tiles)
    rows = lax.broadcasted_iota(jnp.int32, (block, LANES), 0)
    columns = lax.broadcasted_iota(jnp.int32, (block, LANES), 1)
    tile_of_row = jnp.zeros((block, LANES), jnp.int32)
    for t in range(1, tiles + 1):
        tile_of_row = tile_of_row + jnp.where(rows >= t * HARMS, 1, 0)
    harm_of_row = rows - tile_of_row * HARMS
    within = columns
    for n in range(1, SPLITS):
        within = within - jnp.where(columns >= n * used, used, 0)
    harm_of_column = lax.shift_right_logical(within, 3)
    fits_in = jnp.logical_and(
        jnp.logical_and(harm_of_row == harm_of_column, columns < SPLITS * used),
        tile_of_row < tiles,
    )
    station_of_column = lax.bitwise_and(within, stations - 1)
    tile_of_column = jnp.zeros((block, LANES), jnp.int32)
    for s in range(stations):
        tile_of_column = jnp.where(
            station_of_column == s, tile_ref[sta * stations + s], tile_of_column
        )
    pieces = []
    for j in range(sta_count):
        here = jnp.logical_and(fits_in, tile_of_column == tile_of_row + j * tiles)
        pieces.append(jnp.where(here, 1.0, 0.0).astype(f32))
    choose = jnp.concatenate(pieces, axis=0).astype(jnp.bfloat16)

    row = normal_buf[0:1]
    for j in range(1, evt_count):
        normals(j).wait_recv()
        row = row + normal_recv[j - 1, 0:1]
    entries = jnp.broadcast_to(row, (stations, LANES))
    matrix = {}
    place = 0
    for k in range(HARMS):
        for l in range(k + 1):
            value = pick_lanes(entries, TERMS * station_ids + place)
            matrix[k, l] = value + 1.0 if k == l else value
            place += 1
    inverse = []
    ratio = {}
    for p in range(HARMS):
        inverse.append(1.0 / matrix[p, p])
        for k in range(p + 1, HARMS):
            ratio[k, p] = matrix[k, p] * inverse[p]
            for l in range(p + 1, k + 1):
                matrix[k, l] = matrix[k, l] - ratio[k, p] * matrix[l, p]

    part_swap.wait_recv()
    stacked = []
    for z in range(chips):
        right = [
            part_buf[core, z, k * stations:(k + 1) * stations]
            + part_pair[z, k * stations:(k + 1) * stations]
            for k in range(HARMS)
        ]
        for p in range(HARMS):
            for k in range(p + 1, HARMS):
                right[k] = right[k] - ratio[k, p] * right[p]
        solved = [None] * HARMS
        for k in reversed(range(HARMS)):
            value = right[k] * inverse[k]
            for l in range(k + 1, HARMS):
                value = value - ratio[l, k] * solved[l]
            solved[k] = value
        layers = []
        for n in range(SPLITS):
            coarse = [value.astype(jnp.bfloat16).astype(f32) for value in solved]
            layers += coarse
            solved = [value - part for value, part in zip(solved, coarse)]
        layers += [jnp.zeros((stations, LANES), f32)] * (LANES // stations - len(layers))
        stacked.append(jnp.concatenate(layers, axis=0).astype(jnp.bfloat16))
    summed = jnp.dot(
        choose, jnp.concatenate(stacked, axis=1), preferred_element_type=f32
    )
    for z in range(chips):
        for j in range(sta_count):
            tile_buf[z, j] = summed[j * block:(j + 1) * block, z * LANES:(z + 1) * LANES]
    peers(lambda to_sta, to_chip: sums(to_sta, to_chip).start())

    members = jnp.zeros((block, LANES), f32)
    for s in range(sta_count * stations):
        members = members + jnp.where(tile_of_row + sta * tiles == tile_ref[s], 1.0, 0.0)
    scale = 1.0 / jnp.maximum(members, 1.0)

    tile_recv[chip, sta] = tile_buf[chip, sta]
    peers(lambda to_sta, to_chip: sums_from(to_sta, to_chip).wait_recv())
    total = functools.reduce(
        jnp.add, [tile_recv[z, j] for z in range(chips) for j in range(sta_count)]
    )
    total = total * scale
    for t in range(tiles):
        for k in range(HARMS):
            row = total[t * HARMS + k:t * HARMS + k + 1]
            out_ref[t, k, 0:1, :] = row[:, 0:share]
            out_ref[t, k, 1:2, :] = row[:, HALF:HALF + share]
    part_swap.wait_send()
    for j in range(1, evt_count):
        normals(j).wait_send()
    peers(lambda to_sta, to_chip: sums(to_sta, to_chip).wait_send())


def body(evt_count, sta_count, traces, baz_bin, inc_bin, counts, depth_index, tile_of):
    _, stations, slots, samples = traces.shape
    depths = depth_index.shape[1]
    share = depths // evt_count
    chips = evt_count // 2
    pieces = -(-3 * slots // LANES)
    tiles = tile_count(tile_of.shape[0]) // sta_count
    vmem = pl.BlockSpec(memory_space=pltpu.VMEM)
    anywhere = pl.BlockSpec(memory_space=pl.ANY)
    f32 = jnp.float32
    used = HARMS * stations
    return pl.pallas_call(
        functools.partial(kernel, evt_count, sta_count, tiles),
        out_shape=pltpu.VMEM((tiles, HARMS, 2, share), f32),
        in_specs=[anywhere] * 6,
        out_specs=vmem,
        scratch_shapes=[
            pltpu.VMEM((stations, 3, slots, samples), traces.dtype),
            pltpu.VMEM(baz_bin.shape, jnp.int32),
            pltpu.VMEM(inc_bin.shape, jnp.int32),
            pltpu.SMEM(counts.shape, jnp.int32),
            pltpu.VMEM(depth_index.shape, jnp.int32),
            pltpu.SMEM(tile_of.shape, jnp.int32),
            pltpu.VMEM((pieces, 2 * ROWS * stations, LANES), f32),
            pltpu.VMEM((stations, 4 * ROWS, pieces * LANES), jnp.bfloat16),
            pltpu.VMEM((ROWS, LANES), f32),
            pltpu.VMEM((evt_count - 1, ROWS, LANES), f32),
            pltpu.VMEM((stations, samples // LANES * 2 * ROWS, 2 * LANES), jnp.bfloat16),
            pltpu.VMEM((stations, LANES, depths), jnp.bfloat16),
            pltpu.VMEM((2, chips, ROWS * stations, LANES), f32),
            pltpu.VMEM((chips, used, LANES), f32),
            pltpu.VMEM((chips, sta_count, tile_rows(tiles), LANES), f32),
            pltpu.VMEM((chips, sta_count, tile_rows(tiles), LANES), f32),
            pltpu.SemaphoreType.DMA((stations,)),
            pltpu.SemaphoreType.DMA((5,)),
            pltpu.SemaphoreType.DMA((2,)),
            pltpu.SemaphoreType.DMA((evt_count - 1,)),
            pltpu.SemaphoreType.DMA((evt_count - 1,)),
            pltpu.SemaphoreType.DMA((chips, sta_count)),
            pltpu.SemaphoreType.DMA((chips, sta_count)),
        ],
        compiler_params=pltpu.CompilerParams(collective_id=0, has_side_effects=True),
    )(traces, baz_bin, inc_bin, counts, depth_index, tile_of)


def tile_rows(tiles):
    return -(-tiles * HARMS // ROWS) * ROWS


def tile_count(stations):
    return stations // 2


def solution(mesh):
    return jax.shard_map(
        functools.partial(body, mesh.shape["evt"], mesh.shape["sta"]),
        mesh=mesh,
        in_specs=(
            P(None, "sta", "evt", None),
            P("sta", "evt"),
            P("sta", "evt"),
            P("sta"),
            P("sta", None),
            P(),
        ),
        out_specs=P("sta", None, None, "evt"),
        check_vma=False,
    )
```

```python
import functools

import jax
import jax.numpy as jnp
from jax import lax
from jax.experimental import pallas as pl
from jax.experimental.pallas import tpu as pltpu
from jax.sharding import PartitionSpec as P

BAZ_BINS = 36
HARMS = 5
LANES = 128
ROWS = 8
TERMS = 16
HALF = LANES // 2
GROUPS = (4, 4)
SPLITS = 3
MESH = pl.DeviceIdType.MESH


def pick_lanes(values, lanes):
    return jnp.take_along_axis(values, lanes, axis=1, mode="promise_in_bounds")


def groups_of(stations):
    groups, at = [], 0
    while at < stations:
        size = min(GROUPS[len(groups)] if len(groups) < len(GROUPS) else 1, stations - at)
        groups.append(range(at, at + size))
        at += size
    return groups


def kernel(
    evt_count,
    sta_count,
    tiles,
    traces_ref,
    baz_hbm,
    inc_hbm,
    counts_hbm,
    depth_hbm,
    tile_hbm,
    out_ref,
    trace_buf,
    baz_ref,
    inc_ref,
    counts_ref,
    depth_ref,
    tile_ref,
    weight_buf,
    left_buf,
    normal_buf,
    normal_recv,
    split_buf,
    hot_buf,
    part_buf,
    part_pair,
    tile_buf,
    tile_recv,
    load_sem,
    small_sem,
    pair_sem,
    normal_send_sem,
    normal_recv_sem,
    tile_send_sem,
    tile_recv_sem,
    open_sem,
):
    stations, slots = baz_ref.shape
    samples = traces_ref.shape[3]
    depths = depth_ref.shape[1]
    share = depths // evt_count
    used = HARMS * stations
    sent = HARMS * tiles
    evt = lax.axis_index("evt")
    sta = lax.axis_index("sta")
    chips = evt_count // 2
    core = evt % 2
    chip = evt // 2
    partner = {"evt": evt + 1 - 2 * core}
    f32 = jnp.float32

    def load(s):
        return pltpu.make_async_copy(traces_ref.at[:, s], trace_buf.at[s], load_sem.at[s])

    def peers(act):
        def one(n, carry):
            to_chip, to_sta = n // sta_count, n % sta_count

            @pl.when(jnp.logical_or(to_chip != chip, to_sta != sta))
            def _():
                act(to_sta, to_chip)

            return carry

        lax.fori_loop(0, chips * sta_count, one, 0, unroll=chips * sta_count <= 16)

    barrier = pltpu.get_barrier_semaphore()
    for j in range(evt_count - 1, 0, -1):
        pl.semaphore_signal(
            barrier, inc=1, device_id={"evt": lax.rem(evt + j, evt_count)},
            device_id_type=MESH,
        )
    for j in range(1, sta_count):
        pl.semaphore_signal(
            barrier, inc=1, device_id={"sta": lax.rem(sta + j, sta_count)},
            device_id_type=MESH,
        )

    small = [
        pltpu.make_async_copy(src, dst, small_sem.at[n])
        for n, (src, dst) in enumerate(
            [
                (baz_hbm, baz_ref),
                (inc_hbm, inc_ref),
                (counts_hbm, counts_ref),
                (depth_hbm, depth_ref),
                (tile_hbm, tile_ref),
            ]
        )
    ]
    for copy in small:
        copy.start()
    for s in range(stations):
        load(s).start()

    for copy in small:
        copy.wait()

    phi = (baz_ref[...].astype(f32) + 0.5) * (2.0 * jnp.pi / BAZ_BINS)
    tilt = (12.0 + 2.5 * (inc_ref[...].astype(f32) + 0.5)) * (jnp.pi / 180.0)
    cosine, sine = jnp.cos(phi), jnp.sin(phi)
    cos_tilt, sin_tilt = jnp.cos(tilt), jnp.sin(tilt)
    row_ids = lax.broadcasted_iota(jnp.int32, (stations, slots), 0)
    total = jnp.zeros((stations, slots), jnp.int32)
    for s in range(stations):
        total = jnp.where(row_ids == s, counts_ref[s], total)
    slot_ids = evt * slots + lax.broadcasted_iota(jnp.int32, (stations, slots), 1)
    live = jnp.where(slot_ids < total, 1.0, 0.0).astype(f32)
    harm = [
        jnp.ones_like(phi),
        cosine,
        sine,
        2.0 * cosine * cosine - 1.0,
        2.0 * sine * cosine,
    ]
    weighted = [h * live for h in harm]
    parts = [
        [sin_tilt, -cos_tilt * cosine, -cos_tilt * sine],
        [jnp.zeros_like(phi), sine, -cosine],
    ]
    weight_buf[...] = jnp.zeros_like(weight_buf)
    for c in range(2):
        for k in range(HARMS):
            at = (c * ROWS + k) * stations
            for m in range(3):
                lane = m * slots
                weight_buf[
                    lane // LANES, at:at + stations, lane % LANES:lane % LANES + slots
                ] = weighted[k] * parts[c][m]
    for s in range(stations):
        for n in range(weight_buf.shape[0]):
            weights = weight_buf[n, pl.ds(s, 2 * ROWS, stride=stations), :]
            high = weights.astype(jnp.bfloat16)
            low = (weights - high.astype(f32)).astype(jnp.bfloat16)
            left_buf[s, 0:2 * ROWS, n * LANES:(n + 1) * LANES] = high
            left_buf[s, 2 * ROWS:4 * ROWS, n * LANES:(n + 1) * LANES] = low
    lane_ids = lax.broadcasted_iota(jnp.int32, (stations, LANES), 1)
    station_ids = lax.broadcasted_iota(jnp.int32, (stations, LANES), 0)
    packed = jnp.zeros((stations, LANES), f32)
    place = 0
    for k in range(HARMS):
        for l in range(k + 1):
            column = jnp.sum(weighted[k] * harm[l], axis=1, keepdims=True)
            packed = jnp.where(lane_ids % TERMS == place, column, packed)
            place += 1
    packed = jnp.where(lane_ids // TERMS == station_ids, packed, 0.0)
    normal_buf[0:1] = jnp.sum(packed, axis=0, keepdims=True)

    def normals(j):
        return pltpu.make_async_remote_copy(
            src_ref=normal_buf.at[0:1],
            dst_ref=normal_recv.at[j - 1, 0:1],
            send_sem=normal_send_sem.at[j - 1],
            recv_sem=normal_recv_sem.at[j - 1],
            device_id={"evt": lax.rem(evt + j, evt_count)},
            device_id_type=MESH,
        )

    part_swap = pltpu.make_async_remote_copy(
        src_ref=part_buf.at[1 - core, :, 0:used],
        dst_ref=part_pair,
        send_sem=pair_sem.at[0],
        recv_sem=pair_sem.at[1],
        device_id=partner,
        device_id_type=MESH,
    )

    def sums(to_sta, to_chip):
        return pltpu.make_async_remote_copy(
            src_ref=tile_buf.at[to_chip, to_sta, 0:sent],
            dst_ref=tile_recv.at[chip, sta, 0:sent],
            send_sem=tile_send_sem.at[to_chip, to_sta],
            recv_sem=tile_recv_sem.at[chip, sta],
            device_id={"sta": to_sta, "evt": 2 * to_chip + core},
            device_id_type=MESH,
        )

    def sums_from(from_sta, from_chip):
        return pltpu.make_async_remote_copy(
            src_ref=tile_buf.at[from_chip, from_sta, 0:sent],
            dst_ref=tile_recv.at[from_chip, from_sta, 0:sent],
            send_sem=tile_send_sem.at[from_chip, from_sta],
            recv_sem=tile_recv_sem.at[from_chip, from_sta],
            device_id={"sta": from_sta, "evt": 2 * from_chip + core},
            device_id_type=MESH,
        )

    late = 2 * chip >= chips

    def open_up(order):
        pl.semaphore_wait(barrier, evt_count - 1 + sta_count - 1)
        for j in order:
            normals(j).start()
        for j in range(1, sta_count):
            pl.semaphore_signal(
                open_sem, inc=1, device_id={"sta": lax.rem(sta + j, sta_count)},
                device_id_type=MESH,
            )

    @pl.when(late)
    def _():
        open_up(range(1, evt_count))

    lane8 = lax.broadcasted_iota(jnp.int32, (ROWS, LANES), 1)

    parts_of = samples // LANES
    window_ids = lax.broadcasted_iota(jnp.int32, (LANES, depths), 0)

    def right_sides(s):
        block = trace_buf[s].reshape(3 * slots, samples)
        right = jnp.dot(left_buf[s, :, 0:3 * slots], block, preferred_element_type=f32)
        pair = right[0:2 * ROWS] + right[2 * ROWS:4 * ROWS]
        pair = pair + pltpu.roll(pair, samples - 1, 1)
        high = pair.astype(jnp.bfloat16)
        low = (pair - high.astype(f32)).astype(jnp.bfloat16)
        lane = lax.bitwise_and(depth_ref[s:s + 1, :], LANES - 1)
        hot = jnp.where(window_ids == lane, 0.5, 0.0).astype(jnp.bfloat16)
        hot_buf[s] = hot
        for n in range(parts_of):
            at = n * LANES
            split_buf[s, n * 2 * ROWS:(n + 1) * 2 * ROWS, 0:LANES] = high[:, at:at + LANES]
            split_buf[s, n * 2 * ROWS:(n + 1) * 2 * ROWS, LANES:] = low[:, at:at + LANES]

    def pick(s):
        hot = hot_buf[s]
        found = jnp.dot(
            split_buf[s], jnp.concatenate([hot, hot], axis=0), preferred_element_type=f32
        )
        chunk = lax.shift_right_logical(depth_ref[s:s + 1, :], 7)
        chunk = jnp.broadcast_to(chunk, (2 * ROWS, depths))
        got = found[0:2 * ROWS]
        for n in range(1, parts_of):
            got = jnp.where(chunk == n, found[n * 2 * ROWS:(n + 1) * 2 * ROWS], got)
        for z in range(depths // LANES):
            first = got[0:ROWS, z * LANES:(z + 1) * LANES]
            second = got[ROWS:2 * ROWS, z * LANES:(z + 1) * LANES]
            for d in range(LANES // share):
                left = first if d == 0 else pltpu.roll(first, LANES - d * share, 1)
                move = (HALF - d * share) % LANES
                rest = second if move == 0 else pltpu.roll(second, move, 1)
                to = z * (LANES // share) + d
                part_buf[to % 2, to // 2, pl.ds(s, ROWS, stride=stations), :] = jnp.where(
                    lane8 < HALF, left, rest
                )

    groups = groups_of(stations)
    for g, group in enumerate(groups):
        for s in group:
            load(s).wait()
        if g == len(groups) - 1:
            @pl.when(jnp.logical_not(late))
            def _():
                open_up(range(evt_count - 1, 0, -1))

        for s in group:
            right_sides(s)
        if g > 0:
            for s in groups[g - 1]:
                pick(s)
    for s in groups[-1]:
        pick(s)
    part_swap.start()

    block = tile_rows(tiles)
    rows = lax.broadcasted_iota(jnp.int32, (block, LANES), 0)
    columns = lax.broadcasted_iota(jnp.int32, (block, LANES), 1)
    tile_of_row = jnp.zeros((block, LANES), jnp.int32)
    for t in range(1, tiles + 1):
        tile_of_row = tile_of_row + jnp.where(rows >= t * HARMS, 1, 0)
    harm_of_row = rows - tile_of_row * HARMS
    within = columns
    for n in range(1, SPLITS):
        within = within - jnp.where(columns >= n * used, used, 0)
    harm_of_column = lax.shift_right_logical(within, 3)
    fits_in = jnp.logical_and(
        jnp.logical_and(harm_of_row == harm_of_column, columns < SPLITS * used),
        tile_of_row < tiles,
    )
    station_of_column = lax.bitwise_and(within, stations - 1)
    tile_of_column = jnp.zeros((block, LANES), jnp.int32)
    for s in range(stations):
        tile_of_column = jnp.where(
            station_of_column == s, tile_ref[sta * stations + s], tile_of_column
        )
    pieces = []
    for j in range(sta_count):
        here = jnp.logical_and(fits_in, tile_of_column == tile_of_row + j * tiles)
        pieces.append(jnp.where(here, 1.0, 0.0).astype(f32))
    choose = jnp.concatenate(pieces, axis=0).astype(jnp.bfloat16)

    pl.semaphore_wait(open_sem, sta_count - 1)
    for j in range(1, evt_count):
        normals(j).wait_recv()
    row = normal_buf[0:1] + jnp.sum(normal_recv[:, 0:1], axis=0)
    entries = jnp.broadcast_to(row, (stations, LANES))
    matrix = {}
    place = 0
    for k in range(HARMS):
        for l in range(k + 1):
            value = pick_lanes(entries, TERMS * station_ids + place)
            matrix[k, l] = value + 1.0 if k == l else value
            place += 1
    inverse = []
    ratio = {}
    for p in range(HARMS):
        inverse.append(1.0 / matrix[p, p])
        for k in range(p + 1, HARMS):
            ratio[k, p] = matrix[k, p] * inverse[p]
            for l in range(p + 1, k + 1):
                matrix[k, l] = matrix[k, l] - ratio[k, p] * matrix[l, p]

    part_swap.wait_recv()
    stacked = []
    for z in range(chips):
        right = [
            part_buf[core, z, k * stations:(k + 1) * stations]
            + part_pair[z, k * stations:(k + 1) * stations]
            for k in range(HARMS)
        ]
        for p in range(HARMS):
            for k in range(p + 1, HARMS):
                right[k] = right[k] - ratio[k, p] * right[p]
        solved = [None] * HARMS
        for k in reversed(range(HARMS)):
            value = right[k] * inverse[k]
            for l in range(k + 1, HARMS):
                value = value - ratio[l, k] * solved[l]
            solved[k] = value
        layers = []
        for n in range(SPLITS):
            coarse = [value.astype(jnp.bfloat16).astype(f32) for value in solved]
            layers += coarse
            solved = [value - part for value, part in zip(solved, coarse)]
        layers += [jnp.zeros((stations, LANES), f32)] * (LANES // stations - len(layers))
        stacked.append(jnp.concatenate(layers, axis=0).astype(jnp.bfloat16))
    summed = jnp.dot(
        choose, jnp.concatenate(stacked, axis=1), preferred_element_type=f32
    )
    for z in range(chips):
        for j in range(sta_count):
            tile_buf[z, j] = summed[j * block:(j + 1) * block, z * LANES:(z + 1) * LANES]
    peers(lambda to_sta, to_chip: sums(to_sta, to_chip).start())

    members = jnp.zeros((block, LANES), f32)
    for s in range(sta_count * stations):
        members = members + jnp.where(tile_of_row + sta * tiles == tile_ref[s], 1.0, 0.0)
    scale = 1.0 / jnp.maximum(members, 1.0)

    part_swap.wait_send()
    for j in range(1, evt_count):
        normals(j).wait_send()
    peers(lambda to_sta, to_chip: sums(to_sta, to_chip).wait_send())
    tile_recv[chip, sta, 0:sent] = tile_buf[chip, sta, 0:sent]
    peers(lambda to_sta, to_chip: sums_from(to_sta, to_chip).wait_recv())
    total = functools.reduce(
        jnp.add, [tile_recv[z, j, 0:sent] for z in range(chips) for j in range(sta_count)]
    )
    total = total * scale[0:sent]
    for t in range(tiles):
        for k in range(HARMS):
            row = total[t * HARMS + k:t * HARMS + k + 1]
            out_ref[t, k, 0:1, :] = row[:, 0:share]
            out_ref[t, k, 1:2, :] = row[:, HALF:HALF + share]

def body(evt_count, sta_count, traces, baz_bin, inc_bin, counts, depth_index, tile_of):
    _, stations, slots, samples = traces.shape
    depths = depth_index.shape[1]
    share = depths // evt_count
    chips = evt_count // 2
    pieces = -(-3 * slots // LANES)
    tiles = tile_count(tile_of.shape[0]) // sta_count
    vmem = pl.BlockSpec(memory_space=pltpu.VMEM)
    anywhere = pl.BlockSpec(memory_space=pl.ANY)
    f32 = jnp.float32
    used = HARMS * stations
    return pl.pallas_call(
        functools.partial(kernel, evt_count, sta_count, tiles),
        out_shape=pltpu.VMEM((tiles, HARMS, 2, share), f32),
        in_specs=[anywhere] * 6,
        out_specs=vmem,
        scratch_shapes=[
            pltpu.VMEM((stations, 3, slots, samples), traces.dtype),
            pltpu.VMEM(baz_bin.shape, jnp.int32),
            pltpu.VMEM(inc_bin.shape, jnp.int32),
            pltpu.SMEM(counts.shape, jnp.int32),
            pltpu.VMEM(depth_index.shape, jnp.int32),
            pltpu.SMEM(tile_of.shape, jnp.int32),
            pltpu.VMEM((pieces, 2 * ROWS * stations, LANES), f32),
            pltpu.VMEM((stations, 4 * ROWS, pieces * LANES), jnp.bfloat16),
            pltpu.VMEM((ROWS, LANES), f32),
            pltpu.VMEM((evt_count - 1, ROWS, LANES), f32),
            pltpu.VMEM((stations, samples // LANES * 2 * ROWS, 2 * LANES), jnp.bfloat16),
            pltpu.VMEM((stations, LANES, depths), jnp.bfloat16),
            pltpu.VMEM((2, chips, ROWS * stations, LANES), f32),
            pltpu.VMEM((chips, used, LANES), f32),
            pltpu.VMEM((chips, sta_count, tile_rows(tiles), LANES), f32),
            pltpu.VMEM((chips, sta_count, tile_rows(tiles), LANES), f32),
            pltpu.SemaphoreType.DMA((stations,)),
            pltpu.SemaphoreType.DMA((5,)),
            pltpu.SemaphoreType.DMA((2,)),
            pltpu.SemaphoreType.DMA((evt_count - 1,)),
            pltpu.SemaphoreType.DMA((evt_count - 1,)),
            pltpu.SemaphoreType.DMA((chips, sta_count)),
            pltpu.SemaphoreType.DMA((chips, sta_count)),
            pltpu.SemaphoreType.REGULAR,
        ],
        compiler_params=pltpu.CompilerParams(collective_id=0, has_side_effects=True),
    )(traces, baz_bin, inc_bin, counts, depth_index, tile_of)


def tile_rows(tiles):
    return -(-tiles * HARMS // ROWS) * ROWS


def tile_count(stations):
    return stations // 2


def solution(mesh):
    return jax.shard_map(
        functools.partial(body, mesh.shape["evt"], mesh.shape["sta"]),
        mesh=mesh,
        in_specs=(
            P(None, "sta", "evt", None),
            P("sta", "evt"),
            P("sta", "evt"),
            P("sta"),
            P("sta", None),
            P(),
        ),
        out_specs=P("sta", None, None, "evt"),
        check_vma=False,
    )
```

```python
import functools

import jax
import jax.numpy as jnp
from jax import lax
from jax.experimental import pallas as pl
from jax.experimental.pallas import tpu as pltpu
from jax.sharding import PartitionSpec as P

BAZ_BINS = 36
HARMS = 5
LANES = 128
ROWS = 8
TERMS = 16
HALF = LANES // 2
TOP = ROWS - HARMS
PAIR = HARMS - TOP
FOLD = ROWS // PAIR
GROUPS = (4, 4)
SPLITS = 3
MESH = pl.DeviceIdType.MESH


def pick_lanes(values, lanes):
    return jnp.take_along_axis(values, lanes, axis=1, mode="promise_in_bounds")


def positions(c, k):
    if c == 0:
        return [k]
    if k < TOP:
        return [HARMS + k]
    return [ROWS + PAIR * n + HARMS - 1 - k for n in range(ROWS // PAIR)]


def groups_of(stations):
    groups, at = [], 0
    while at < stations:
        size = min(GROUPS[len(groups)] if len(groups) < len(GROUPS) else 1, stations - at)
        groups.append(range(at, at + size))
        at += size
    return groups


def kernel(
    evt_count,
    sta_count,
    tiles,
    traces_ref,
    baz_hbm,
    inc_hbm,
    counts_hbm,
    depth_hbm,
    tile_hbm,
    out_ref,
    trace_buf,
    baz_ref,
    inc_ref,
    counts_ref,
    depth_ref,
    tile_ref,
    weight_buf,
    left_buf,
    normal_buf,
    normal_recv,
    split_buf,
    hot_buf,
    part_buf,
    part_pair,
    tile_buf,
    tile_recv,
    far_recv,
    far_normal,
    far_sum,
    load_sem,
    small_sem,
    pair_sem,
    normal_send_sem,
    normal_recv_sem,
    tile_send_sem,
    tile_recv_sem,
    open_sem,
    far_send_sem,
    far_recv_sem,
    far_normal_sem,
):
    stations, slots = baz_ref.shape
    samples = traces_ref.shape[3]
    depths = depth_ref.shape[1]
    share = depths // evt_count
    used = HARMS * stations
    sent = HARMS * tiles
    evt = lax.axis_index("evt")
    sta = lax.axis_index("sta")
    chips = evt_count // 2
    core = evt % 2
    chip = evt // 2
    partner = {"evt": evt + 1 - 2 * core}
    f32 = jnp.float32

    def load(s):
        return pltpu.make_async_copy(traces_ref.at[:, s], trace_buf.at[s], load_sem.at[s])

    def peers(act):
        def one(n, carry):
            to_chip, to_sta = n // sta_count, n % sta_count

            @pl.when(jnp.logical_or(to_chip != chip, to_sta != sta))
            def _():
                act(to_sta, to_chip)

            return carry

        lax.fori_loop(0, chips * sta_count, one, 0, unroll=chips * sta_count <= 16)

    barrier = pltpu.get_barrier_semaphore()
    for j in range(1, evt_count):
        pl.semaphore_signal(
            barrier, inc=1, device_id={"evt": lax.rem(evt + j, evt_count)},
            device_id_type=MESH,
        )
    for j in range(1, sta_count):
        pl.semaphore_signal(
            barrier, inc=1, device_id={"sta": lax.rem(sta + j, sta_count)},
            device_id_type=MESH,
        )

    is_first = jnp.logical_and(evt == 0, sta == 0)
    no_mate = jnp.logical_and(evt != 0, sta != 0)

    @pl.when(is_first)
    def _():
        for j in range(1, sta_count):
            for n in range(1, evt_count):
                pl.semaphore_signal(
                    barrier, inc=1, device_id={"sta": j, "evt": n}, device_id_type=MESH
                )

    small = [
        pltpu.make_async_copy(src, dst, small_sem.at[n])
        for n, (src, dst) in enumerate(
            [
                (baz_hbm, baz_ref),
                (inc_hbm, inc_ref),
                (counts_hbm, counts_ref),
                (depth_hbm, depth_ref),
                (tile_hbm, tile_ref),
            ]
        )
    ]
    for copy in small:
        copy.start()
    for s in range(stations):
        load(s).start()

    for copy in small:
        copy.wait()

    phi = (baz_ref[...].astype(f32) + 0.5) * (2.0 * jnp.pi / BAZ_BINS)
    tilt = (12.0 + 2.5 * (inc_ref[...].astype(f32) + 0.5)) * (jnp.pi / 180.0)
    cosine, sine = jnp.cos(phi), jnp.sin(phi)
    cos_tilt, sin_tilt = jnp.cos(tilt), jnp.sin(tilt)
    row_ids = lax.broadcasted_iota(jnp.int32, (stations, slots), 0)
    total = jnp.zeros((stations, slots), jnp.int32)
    for s in range(stations):
        total = jnp.where(row_ids == s, counts_ref[s], total)
    slot_ids = evt * slots + lax.broadcasted_iota(jnp.int32, (stations, slots), 1)
    live = jnp.where(slot_ids < total, 1.0, 0.0).astype(f32)
    harm = [
        jnp.ones_like(phi),
        cosine,
        sine,
        2.0 * cosine * cosine - 1.0,
        2.0 * sine * cosine,
    ]
    weighted = [h * live for h in harm]
    lane_ids = lax.broadcasted_iota(jnp.int32, (stations, LANES), 1)
    station_ids = lax.broadcasted_iota(jnp.int32, (stations, LANES), 0)
    packed = jnp.zeros((stations, LANES), f32)
    place = 0
    for k in range(HARMS):
        for l in range(k + 1):
            column = jnp.sum(weighted[k] * harm[l], axis=1, keepdims=True)
            packed = jnp.where(lane_ids % TERMS == place, column, packed)
            place += 1
    packed = jnp.where(lane_ids // TERMS == station_ids, packed, 0.0)
    normal_buf[0:1] = jnp.sum(packed, axis=0, keepdims=True)

    def normals(j):
        return pltpu.make_async_remote_copy(
            src_ref=normal_buf.at[0:1],
            dst_ref=normal_recv.at[j - 1, 0:1],
            send_sem=normal_send_sem.at[j - 1],
            recv_sem=normal_recv_sem.at[j - 1],
            device_id={"evt": lax.rem(evt + j, evt_count)},
            device_id_type=MESH,
        )

    part_swap = pltpu.make_async_remote_copy(
        src_ref=part_buf.at[1 - core, :, 0:used],
        dst_ref=part_pair,
        send_sem=pair_sem.at[0],
        recv_sem=pair_sem.at[1],
        device_id=partner,
        device_id_type=MESH,
    )

    def sums(to_sta, to_chip):
        return pltpu.make_async_remote_copy(
            src_ref=tile_buf.at[to_chip, to_sta, 0:sent],
            dst_ref=tile_recv.at[chip, sta, 0:sent],
            send_sem=tile_send_sem.at[to_chip, to_sta],
            recv_sem=tile_recv_sem.at[chip, sta],
            device_id={"sta": to_sta, "evt": 2 * to_chip + core},
            device_id_type=MESH,
        )

    def far(from_sta, from_evt):
        return pltpu.make_async_remote_copy(
            src_ref=part_buf.at[0, 0, 0:used],
            dst_ref=far_recv.at[from_sta, from_evt],
            send_sem=far_send_sem.at[0],
            recv_sem=far_recv_sem.at[from_sta, from_evt],
            device_id={"sta": 0, "evt": 0},
            device_id_type=MESH,
        )

    def far_row(from_sta, from_evt):
        return pltpu.make_async_remote_copy(
            src_ref=normal_buf.at[0:1],
            dst_ref=far_normal.at[from_sta, from_evt, 0:1],
            send_sem=far_send_sem.at[1],
            recv_sem=far_normal_sem.at[from_sta, from_evt],
            device_id={"sta": 0, "evt": 0},
            device_id_type=MESH,
        )

    def sums_from(from_sta, from_chip):
        return pltpu.make_async_remote_copy(
            src_ref=tile_buf.at[from_chip, from_sta, 0:sent],
            dst_ref=tile_recv.at[from_chip, from_sta, 0:sent],
            send_sem=tile_send_sem.at[from_chip, from_sta],
            recv_sem=tile_recv_sem.at[from_chip, from_sta],
            device_id={"sta": from_sta, "evt": 2 * from_chip + core},
            device_id_type=MESH,
        )

    late = 2 * chip >= chips

    def is_sent(to_sta, to_chip):
        return jnp.logical_or(to_sta != 0, jnp.logical_or(to_chip != 0, core != 0))

    def open_up(order):
        pl.semaphore_wait(barrier, evt_count - 1 + sta_count - 1 + jnp.where(no_mate, 1, 0))

        @pl.when(sta != 0)
        def _():
            far_row(sta, evt).start()

        for j in order:
            normals(j).start()
        for j in range(1, sta_count):
            pl.semaphore_signal(
                open_sem, inc=1, device_id={"sta": lax.rem(sta + j, sta_count)},
                device_id_type=MESH,
            )

    @pl.when(late)
    def _():
        open_up(range(1, evt_count))

    parts = [
        [sin_tilt, -cos_tilt * cosine, -cos_tilt * sine],
        [jnp.zeros_like(phi), sine, -cosine],
    ]
    weight_buf[...] = jnp.zeros_like(weight_buf)
    for c in range(2):
        for k in range(HARMS):
            for m in range(3):
                lane = m * slots
                weight = weighted[k] * parts[c][m]
                for position in positions(c, k):
                    at = position * stations
                    weight_buf[
                        lane // LANES, at:at + stations, lane % LANES:lane % LANES + slots
                    ] = weight
    for s in range(stations):
        for n in range(weight_buf.shape[0]):
            weights = weight_buf[n, pl.ds(s, 2 * ROWS, stride=stations), :]
            high = weights.astype(jnp.bfloat16)
            low = (weights - high.astype(f32)).astype(jnp.bfloat16)
            left_buf[s, 0:2 * ROWS, n * LANES:(n + 1) * LANES] = high
            left_buf[s, 2 * ROWS:4 * ROWS, n * LANES:(n + 1) * LANES] = low

    lane8 = lax.broadcasted_iota(jnp.int32, (ROWS, LANES), 1)
    row8 = lax.broadcasted_iota(jnp.int32, (ROWS, LANES), 0)

    parts_of = samples // LANES
    window_ids = lax.broadcasted_iota(jnp.int32, (LANES, depths), 0)

    def right_sides(s):
        block = trace_buf[s].reshape(3 * slots, samples)
        right = jnp.dot(left_buf[s, :, 0:3 * slots], block, preferred_element_type=f32)
        pair = right[0:2 * ROWS] + right[2 * ROWS:4 * ROWS]
        pair = pair + pltpu.roll(pair, samples - 1, 1)
        blocks = []
        for q in range(0, parts_of, FOLD):
            rest = pair[ROWS:2 * ROWS, q * LANES:(q + 1) * LANES]
            for n in range(FOLD):
                part = pair[:, (q + n) * LANES:(q + n + 1) * LANES]
                blocks.append(part[0:ROWS])
                if n:
                    rest = jnp.where(row8 // PAIR == n, part[ROWS:2 * ROWS], rest)
            blocks.append(rest)
        stacked = jnp.concatenate(blocks, axis=0)
        high = stacked.astype(jnp.bfloat16)
        split_buf[s, :, 0:LANES] = high
        split_buf[s, :, LANES:] = (stacked - high.astype(f32)).astype(jnp.bfloat16)
        lane = lax.bitwise_and(depth_ref[s:s + 1, :], LANES - 1)
        hot = jnp.where(window_ids == lane, 0.5, 0.0).astype(jnp.bfloat16)
        hot_buf[s] = hot

    def pick(s):
        hot = hot_buf[s]
        found = jnp.dot(
            split_buf[s], jnp.concatenate([hot, hot], axis=0), preferred_element_type=f32
        )
        chunk = lax.shift_right_logical(depth_ref[s:s + 1, :], 7)
        for z in range(depths // LANES):
            here = slice(z * LANES, (z + 1) * LANES)
            part = jnp.broadcast_to(chunk[:, here], (ROWS, LANES))
            first = found[0:ROWS, here]
            rest = found[FOLD * ROWS:(FOLD + 1) * ROWS, here]
            for n in range(1, parts_of):
                at = (n // FOLD * (FOLD + 1) + n % FOLD) * ROWS
                first = jnp.where(part == n, found[at:at + ROWS, here], first)
                if n % FOLD == 0:
                    at = at + FOLD * ROWS
                    rest = jnp.where(part >= n, found[at:at + ROWS, here], rest)
            rest = jnp.where(row8 // PAIR == part % FOLD, rest, 0.0)
            turn = PAIR
            while turn < ROWS:
                rest = rest + pltpu.roll(rest, turn, 0)
                turn *= 2
            second = jnp.where(row8 < TOP, pltpu.roll(first, ROWS - HARMS, 0), rest)
            for d in range(LANES // share):
                left = first if d == 0 else pltpu.roll(first, LANES - d * share, 1)
                move = (HALF - d * share) % LANES
                rest = second if move == 0 else pltpu.roll(second, move, 1)
                to = z * (LANES // share) + d
                part_buf[to % 2, to // 2, pl.ds(s, ROWS, stride=stations), :] = jnp.where(
                    lane8 < HALF, left, rest
                )

    groups = groups_of(stations)
    for g, group in enumerate(groups):
        for s in group:
            load(s).wait()
        if g == len(groups) - 1:
            @pl.when(jnp.logical_not(late))
            def _():
                open_up(range(evt_count - 1, 0, -1))


        before = list(groups[g - 1]) if g else []
        for n, s in enumerate(group):
            right_sides(s)
            if n < len(before):
                pick(before[n])
        for s in before[len(group):]:
            pick(s)
    for s in groups[-1]:
        pick(s)
    @pl.when(jnp.logical_not(is_first))
    def _():
        far(sta, evt).start()

    part_swap.start()

    block = tile_rows(tiles)
    rows = lax.broadcasted_iota(jnp.int32, (block, LANES), 0)
    columns = lax.broadcasted_iota(jnp.int32, (block, LANES), 1)
    tile_of_row = jnp.zeros((block, LANES), jnp.int32)
    for t in range(1, tiles + 1):
        tile_of_row = tile_of_row + jnp.where(rows >= t * HARMS, 1, 0)
    harm_of_row = rows - tile_of_row * HARMS
    within = columns
    for n in range(1, SPLITS):
        within = within - jnp.where(columns >= n * used, used, 0)
    harm_of_column = lax.shift_right_logical(within, 3)
    fits_in = jnp.logical_and(
        jnp.logical_and(harm_of_row == harm_of_column, columns < SPLITS * used),
        tile_of_row < tiles,
    )
    station_of_column = lax.bitwise_and(within, stations - 1)
    tile_of_column = jnp.zeros((block, LANES), jnp.int32)
    for s in range(stations):
        tile_of_column = jnp.where(
            station_of_column == s, tile_ref[sta * stations + s], tile_of_column
        )
    pieces = []
    for j in range(sta_count):
        here = jnp.logical_and(fits_in, tile_of_column == tile_of_row + j * tiles)
        pieces.append(jnp.where(here, 1.0, 0.0).astype(f32))
    choose = jnp.concatenate(pieces, axis=0).astype(jnp.bfloat16)

    pl.semaphore_wait(open_sem, sta_count - 1)
    for j in range(1, evt_count):
        normals(j).wait_recv()
    row = normal_buf[0:1] + jnp.sum(normal_recv[:, 0:1], axis=0)
    def factor(row):
        entries = jnp.broadcast_to(row, (stations, LANES))
        matrix = {}
        place = 0
        for k in range(HARMS):
            for l in range(k + 1):
                value = pick_lanes(entries, TERMS * station_ids + place)
                matrix[k, l] = value + 1.0 if k == l else value
                place += 1
        inverse = []
        ratio = {}
        for p in range(HARMS):
            inverse.append(1.0 / matrix[p, p])
            for k in range(p + 1, HARMS):
                ratio[k, p] = matrix[k, p] * inverse[p]
                for l in range(p + 1, k + 1):
                    matrix[k, l] = matrix[k, l] - ratio[k, p] * matrix[l, p]
        return inverse, ratio

    def solve(right, inverse, ratio):
        right = list(right)
        for p in range(HARMS):
            for k in range(p + 1, HARMS):
                right[k] = right[k] - ratio[k, p] * right[p]
        solved = [None] * HARMS
        for k in reversed(range(HARMS)):
            value = right[k] * inverse[k]
            for l in range(k + 1, HARMS):
                value = value - ratio[l, k] * solved[l]
            solved[k] = value
        layers = []
        for n in range(SPLITS):
            coarse = [value.astype(jnp.bfloat16).astype(f32) for value in solved]
            layers += coarse
            solved = [value - part for value, part in zip(solved, coarse)]
        layers += [jnp.zeros((stations, LANES), f32)] * (LANES // stations - len(layers))
        return jnp.concatenate(layers, axis=0).astype(jnp.bfloat16)

    normal_buf[1:2] = row
    inverse, ratio = factor(row)

    part_swap.wait_recv()
    stacked = []
    for z in range(chips):
        right = [
            part_buf[core, z, k * stations:(k + 1) * stations]
            + part_pair[z, k * stations:(k + 1) * stations]
            for k in range(HARMS)
        ]
        stacked.append(solve(right, inverse, ratio))
    summed = jnp.dot(
        choose, jnp.concatenate(stacked, axis=1), preferred_element_type=f32
    )
    for z in range(chips):
        for j in range(sta_count):
            tile_buf[z, j] = summed[j * block:(j + 1) * block, z * LANES:(z + 1) * LANES]

    def send(to_sta, to_chip):
        @pl.when(is_sent(to_sta, to_chip))
        def _():
            sums(to_sta, to_chip).start()

    peers(send)

    members = jnp.zeros((block, LANES), f32)
    for s in range(sta_count * stations):
        members = members + jnp.where(tile_of_row + sta * tiles == tile_ref[s], 1.0, 0.0)
    scale = 1.0 / jnp.maximum(members, 1.0)

    part_swap.wait_send()
    for j in range(1, evt_count):
        normals(j).wait_send()

    def sent_out(to_sta, to_chip):
        @pl.when(is_sent(to_sta, to_chip))
        def _():
            sums(to_sta, to_chip).wait_send()

    peers(sent_out)

    @pl.when(jnp.logical_not(is_first))
    def _():
        far(sta, evt).wait_send()

    @pl.when(sta != 0)
    def _():
        far_row(sta, evt).wait_send()

    tile_recv[chip, sta] = tile_buf[chip, sta]
    @pl.when(is_first)
    def _():
        for j in range(1, sta_count):
            for n in range(evt_count):
                far_row(j, n).wait_recv()
        factors = [factor(normal_buf[1:2])]
        for j in range(1, sta_count):
            factors.append(factor(jnp.sum(far_normal[j, :, 0:1], axis=0)))
        chosen = []
        for j in range(sta_count):
            of = jnp.zeros((block, LANES), jnp.int32)
            for s in range(stations):
                of = jnp.where(station_of_column == s, tile_ref[j * stations + s], of)
            here = jnp.logical_and(fits_in, of == tile_of_row)
            chosen.append(jnp.where(here, 1.0, 0.0).astype(jnp.bfloat16))
        layers = []
        for j in range(sta_count):
            for n in range(evt_count):
                if j or n:
                    far(j, n).wait_recv()
            right = []
            for k in range(HARMS):
                at = slice(k * stations, (k + 1) * stations)
                terms = [far_recv[j, n, at] for n in range(evt_count) if j or n]
                if j == 0:
                    terms.append(part_buf[0, 0, at])
                right.append(functools.reduce(jnp.add, terms))
            layers.append(solve(right, *factors[j]))
        far_sum[...] = functools.reduce(
            jnp.add,
            [
                jnp.dot(left, right, preferred_element_type=f32)
                for left, right in zip(chosen, layers)
            ],
        )


    @pl.when(jnp.logical_not(is_first))
    def _():
        peers(lambda from_sta, from_chip: sums_from(from_sta, from_chip).wait_recv())
        far_sum[0:sent] = functools.reduce(
            jnp.add, [tile_recv[z, j, 0:sent] for z in range(chips) for j in range(sta_count)]
        )

    total = far_sum[0:sent]
    total = total * scale[0:sent]
    for t in range(tiles):
        for k in range(HARMS):
            row = total[t * HARMS + k:t * HARMS + k + 1]
            out_ref[t, k, 0:1, :] = row[:, 0:share]
            out_ref[t, k, 1:2, :] = row[:, HALF:HALF + share]

def body(evt_count, sta_count, traces, baz_bin, inc_bin, counts, depth_index, tile_of):
    _, stations, slots, samples = traces.shape
    depths = depth_index.shape[1]
    share = depths // evt_count
    chips = evt_count // 2
    pieces = -(-3 * slots // LANES)
    tiles = tile_count(tile_of.shape[0]) // sta_count
    vmem = pl.BlockSpec(memory_space=pltpu.VMEM)
    anywhere = pl.BlockSpec(memory_space=pl.ANY)
    f32 = jnp.float32
    used = HARMS * stations
    return pl.pallas_call(
        functools.partial(kernel, evt_count, sta_count, tiles),
        out_shape=pltpu.VMEM((tiles, HARMS, 2, share), f32),
        in_specs=[anywhere] * 6,
        out_specs=vmem,
        scratch_shapes=[
            pltpu.VMEM((stations, 3, slots, samples), traces.dtype),
            pltpu.VMEM(baz_bin.shape, jnp.int32),
            pltpu.VMEM(inc_bin.shape, jnp.int32),
            pltpu.SMEM(counts.shape, jnp.int32),
            pltpu.VMEM(depth_index.shape, jnp.int32),
            pltpu.SMEM(tile_of.shape, jnp.int32),
            pltpu.VMEM((pieces, 2 * ROWS * stations, LANES), f32),
            pltpu.VMEM((stations, 4 * ROWS, pieces * LANES), jnp.bfloat16),
            pltpu.VMEM((ROWS, LANES), f32),
            pltpu.VMEM((evt_count - 1, ROWS, LANES), f32),
            pltpu.VMEM((stations, samples // LANES * 2 * HARMS, 2 * LANES), jnp.bfloat16),
            pltpu.VMEM((stations, LANES, depths), jnp.bfloat16),
            pltpu.VMEM((2, chips, ROWS * stations, LANES), f32),
            pltpu.VMEM((chips, used, LANES), f32),
            pltpu.VMEM((chips, sta_count, tile_rows(tiles), LANES), f32),
            pltpu.VMEM((chips, sta_count, tile_rows(tiles), LANES), f32),
            pltpu.VMEM((sta_count, evt_count, used, LANES), f32),
            pltpu.VMEM((sta_count, evt_count, ROWS, LANES), f32),
            pltpu.VMEM((tile_rows(tiles), LANES), f32),
            pltpu.SemaphoreType.DMA((stations,)),
            pltpu.SemaphoreType.DMA((5,)),
            pltpu.SemaphoreType.DMA((2,)),
            pltpu.SemaphoreType.DMA((evt_count - 1,)),
            pltpu.SemaphoreType.DMA((evt_count - 1,)),
            pltpu.SemaphoreType.DMA((chips, sta_count)),
            pltpu.SemaphoreType.DMA((chips, sta_count)),
            pltpu.SemaphoreType.REGULAR,
            pltpu.SemaphoreType.DMA((2,)),
            pltpu.SemaphoreType.DMA((sta_count, evt_count)),
            pltpu.SemaphoreType.DMA((sta_count, evt_count)),
        ],
        compiler_params=pltpu.CompilerParams(collective_id=0, has_side_effects=True),
    )(traces, baz_bin, inc_bin, counts, depth_index, tile_of)


def tile_rows(tiles):
    return -(-tiles * HARMS // ROWS) * ROWS


def tile_count(stations):
    return stations // 2


def solution(mesh):
    return jax.shard_map(
        functools.partial(body, mesh.shape["evt"], mesh.shape["sta"]),
        mesh=mesh,
        in_specs=(
            P(None, "sta", "evt", None),
            P("sta", "evt"),
            P("sta", "evt"),
            P("sta"),
            P("sta", None),
            P(),
        ),
        out_specs=P("sta", None, None, "evt"),
        check_vma=False,
    )
```

```python
import functools

import jax
import jax.numpy as jnp
from jax import lax
from jax.experimental import pallas as pl
from jax.experimental.pallas import tpu as pltpu
from jax.sharding import PartitionSpec as P

BAZ_BINS = 36
HARMS = 5
LANES = 128
ROWS = 8
TERMS = 16
HALF = LANES // 2
TOP = ROWS - HARMS
PAIR = HARMS - TOP
FOLD = ROWS // PAIR
GROUPS = (4, 4)
SPLITS = 3
MESH = pl.DeviceIdType.MESH


def pick_lanes(values, lanes):
    return jnp.take_along_axis(values, lanes, axis=1, mode="promise_in_bounds")


def positions(c, k):
    if c == 0:
        return [k]
    if k < TOP:
        return [HARMS + k]
    return [ROWS + PAIR * n + HARMS - 1 - k for n in range(ROWS // PAIR)]


def groups_of(stations):
    groups, at = [], 0
    while at < stations:
        size = min(GROUPS[len(groups)] if len(groups) < len(GROUPS) else 1, stations - at)
        groups.append(range(at, at + size))
        at += size
    return groups


def kernel(
    evt_count,
    sta_count,
    tiles,
    traces_ref,
    baz_hbm,
    inc_hbm,
    counts_hbm,
    depth_hbm,
    tile_hbm,
    out_ref,
    trace_buf,
    baz_ref,
    inc_ref,
    counts_ref,
    depth_ref,
    tile_ref,
    weight_buf,
    left_buf,
    normal_buf,
    normal_recv,
    split_buf,
    hot_buf,
    part_buf,
    part_pair,
    tile_buf,
    tile_recv,
    far_recv,
    far_normal,
    far_sum,
    load_sem,
    small_sem,
    pair_sem,
    normal_send_sem,
    normal_recv_sem,
    tile_send_sem,
    tile_recv_sem,
    open_sem,
    far_send_sem,
    far_recv_sem,
    far_normal_sem,
):
    stations, slots = baz_ref.shape
    samples = traces_ref.shape[3]
    depths = depth_ref.shape[1]
    share = depths // evt_count
    used = HARMS * stations
    sent = HARMS * tiles
    evt = lax.axis_index("evt")
    sta = lax.axis_index("sta")
    chips = evt_count // 2
    core = evt % 2
    chip = evt // 2
    partner = {"evt": evt + 1 - 2 * core}
    f32 = jnp.float32

    def load(s):
        return pltpu.make_async_copy(traces_ref.at[:, s], trace_buf.at[s], load_sem.at[s])

    def peers(act):
        def one(n, carry):
            to_chip, to_sta = n // sta_count, n % sta_count

            @pl.when(jnp.logical_or(to_chip != chip, to_sta != sta))
            def _():
                act(to_sta, to_chip)

            return carry

        lax.fori_loop(0, chips * sta_count, one, 0, unroll=chips * sta_count <= 16)

    barrier = pltpu.get_barrier_semaphore()
    for j in range(1, evt_count):
        pl.semaphore_signal(
            barrier, inc=1, device_id={"evt": lax.rem(evt + j, evt_count)},
            device_id_type=MESH,
        )
    for j in range(1, sta_count):
        pl.semaphore_signal(
            barrier, inc=1, device_id={"sta": lax.rem(sta + j, sta_count)},
            device_id_type=MESH,
        )

    is_first = jnp.logical_and(evt == 0, sta == 0)
    no_mate = jnp.logical_and(evt != 0, sta != 0)

    @pl.when(is_first)
    def _():
        for j in range(1, sta_count):
            for n in range(1, evt_count):
                pl.semaphore_signal(
                    barrier, inc=1, device_id={"sta": j, "evt": n}, device_id_type=MESH
                )

    small = [
        pltpu.make_async_copy(src, dst, small_sem.at[n])
        for n, (src, dst) in enumerate(
            [
                (baz_hbm, baz_ref),
                (inc_hbm, inc_ref),
                (counts_hbm, counts_ref),
                (depth_hbm, depth_ref),
                (tile_hbm, tile_ref),
            ]
        )
    ]
    for copy in small:
        copy.start()
    for s in range(stations):
        load(s).start()

    for copy in small:
        copy.wait()

    phi = (baz_ref[...].astype(f32) + 0.5) * (2.0 * jnp.pi / BAZ_BINS)
    tilt = (12.0 + 2.5 * (inc_ref[...].astype(f32) + 0.5)) * (jnp.pi / 180.0)
    cosine, sine = jnp.cos(phi), jnp.sin(phi)
    cos_tilt, sin_tilt = jnp.cos(tilt), jnp.sin(tilt)
    row_ids = lax.broadcasted_iota(jnp.int32, (stations, slots), 0)
    total = jnp.zeros((stations, slots), jnp.int32)
    for s in range(stations):
        total = jnp.where(row_ids == s, counts_ref[s], total)
    slot_ids = evt * slots + lax.broadcasted_iota(jnp.int32, (stations, slots), 1)
    live = jnp.where(slot_ids < total, 1.0, 0.0).astype(f32)
    harm = [
        jnp.ones_like(phi),
        cosine,
        sine,
        2.0 * cosine * cosine - 1.0,
        2.0 * sine * cosine,
    ]
    weighted = [h * live for h in harm]
    lane_ids = lax.broadcasted_iota(jnp.int32, (stations, LANES), 1)
    station_ids = lax.broadcasted_iota(jnp.int32, (stations, LANES), 0)
    packed = jnp.zeros((stations, LANES), f32)
    place = 0
    for k in range(HARMS):
        for l in range(k + 1):
            column = jnp.sum(weighted[k] * harm[l], axis=1, keepdims=True)
            packed = jnp.where(lane_ids % TERMS == place, column, packed)
            place += 1
    packed = jnp.where(lane_ids // TERMS == station_ids, packed, 0.0)
    normal_buf[0:1] = jnp.sum(packed, axis=0, keepdims=True)

    def normals(j):
        return pltpu.make_async_remote_copy(
            src_ref=normal_buf.at[0:1],
            dst_ref=normal_recv.at[j - 1, 0:1],
            send_sem=normal_send_sem.at[j - 1],
            recv_sem=normal_recv_sem.at[j - 1],
            device_id={"evt": lax.rem(evt + j, evt_count)},
            device_id_type=MESH,
        )

    part_swap = pltpu.make_async_remote_copy(
        src_ref=part_buf.at[1 - core, :, 0:used],
        dst_ref=part_pair,
        send_sem=pair_sem.at[0],
        recv_sem=pair_sem.at[1],
        device_id=partner,
        device_id_type=MESH,
    )

    def sums(to_sta, to_chip):
        return pltpu.make_async_remote_copy(
            src_ref=tile_buf.at[to_chip, to_sta, 0:sent],
            dst_ref=tile_recv.at[chip, sta, 0:sent],
            send_sem=tile_send_sem.at[to_chip, to_sta],
            recv_sem=tile_recv_sem.at[chip, sta],
            device_id={"sta": to_sta, "evt": 2 * to_chip + core},
            device_id_type=MESH,
        )

    def far(from_sta, from_evt):
        return pltpu.make_async_remote_copy(
            src_ref=part_buf.at[0, 0, 0:used],
            dst_ref=far_recv.at[from_sta, from_evt],
            send_sem=far_send_sem.at[0],
            recv_sem=far_recv_sem.at[from_sta, from_evt],
            device_id={"sta": 0, "evt": 0},
            device_id_type=MESH,
        )

    def far_row(from_sta, from_evt):
        return pltpu.make_async_remote_copy(
            src_ref=normal_buf.at[0:1],
            dst_ref=far_normal.at[from_sta, from_evt, 0:1],
            send_sem=far_send_sem.at[1],
            recv_sem=far_normal_sem.at[from_sta, from_evt],
            device_id={"sta": 0, "evt": 0},
            device_id_type=MESH,
        )

    def sums_from(from_sta, from_chip):
        return pltpu.make_async_remote_copy(
            src_ref=tile_buf.at[from_chip, from_sta, 0:sent],
            dst_ref=tile_recv.at[from_chip, from_sta, 0:sent],
            send_sem=tile_send_sem.at[from_chip, from_sta],
            recv_sem=tile_recv_sem.at[from_chip, from_sta],
            device_id={"sta": from_sta, "evt": 2 * from_chip + core},
            device_id_type=MESH,
        )

    late = 2 * chip >= chips

    def is_sent(to_sta, to_chip):
        return jnp.logical_or(to_sta != 0, jnp.logical_or(to_chip != 0, core != 0))

    def open_up(order):
        pl.semaphore_wait(barrier, evt_count - 1 + sta_count - 1 + jnp.where(no_mate, 1, 0))

        @pl.when(sta != 0)
        def _():
            far_row(sta, evt).start()

        for j in order:
            normals(j).start()
        for j in range(1, sta_count):
            pl.semaphore_signal(
                open_sem, inc=1, device_id={"sta": lax.rem(sta + j, sta_count)},
                device_id_type=MESH,
            )

    @pl.when(late)
    def _():
        open_up(range(1, evt_count))

    parts = [
        [sin_tilt, -cos_tilt * cosine, -cos_tilt * sine],
        [jnp.zeros_like(phi), sine, -cosine],
    ]
    weight_buf[...] = jnp.zeros_like(weight_buf)
    for c in range(2):
        for k in range(HARMS):
            for m in range(3):
                lane = m * slots
                weight = weighted[k] * parts[c][m]
                for position in positions(c, k):
                    at = position * stations
                    weight_buf[
                        lane // LANES, at:at + stations, lane % LANES:lane % LANES + slots
                    ] = weight
    for s in range(stations):
        for n in range(weight_buf.shape[0]):
            weights = weight_buf[n, pl.ds(s, 2 * ROWS, stride=stations), :]
            high = weights.astype(jnp.bfloat16)
            low = (weights - high.astype(f32)).astype(jnp.bfloat16)
            left_buf[s, 0:2 * ROWS, n * LANES:(n + 1) * LANES] = high
            left_buf[s, 2 * ROWS:4 * ROWS, n * LANES:(n + 1) * LANES] = low

    lane8 = lax.broadcasted_iota(jnp.int32, (ROWS, LANES), 1)
    row8 = lax.broadcasted_iota(jnp.int32, (ROWS, LANES), 0)

    parts_of = samples // LANES
    window_ids = lax.broadcasted_iota(jnp.int32, (LANES, depths), 0)

    def right_sides(s):
        block = trace_buf[s].reshape(3 * slots, samples)
        right = jnp.dot(left_buf[s, :, 0:3 * slots], block, preferred_element_type=f32)
        pair = right[0:2 * ROWS] + right[2 * ROWS:4 * ROWS]
        pair = pair + pltpu.roll(pair, samples - 1, 1)
        blocks = []
        for q in range(0, parts_of, FOLD):
            rest = pair[ROWS:2 * ROWS, q * LANES:(q + 1) * LANES]
            for n in range(FOLD):
                part = pair[:, (q + n) * LANES:(q + n + 1) * LANES]
                blocks.append(part[0:ROWS])
                if n:
                    rest = jnp.where(row8 // PAIR == n, part[ROWS:2 * ROWS], rest)
            blocks.append(rest)
        stacked = jnp.concatenate(blocks, axis=0)
        high = stacked.astype(jnp.bfloat16)
        split_buf[s, :, 0:LANES] = high
        split_buf[s, :, LANES:] = (stacked - high.astype(f32)).astype(jnp.bfloat16)
        lane = lax.bitwise_and(depth_ref[s:s + 1, :], LANES - 1)
        hot = jnp.where(window_ids == lane, 0.5, 0.0).astype(jnp.bfloat16)
        hot_buf[s] = hot

    def pick(s):
        hot = hot_buf[s]
        found = jnp.dot(
            split_buf[s], jnp.concatenate([hot, hot], axis=0), preferred_element_type=f32
        )
        chunk = lax.shift_right_logical(depth_ref[s:s + 1, :], 7)
        for z in range(depths // LANES):
            here = slice(z * LANES, (z + 1) * LANES)
            part = jnp.broadcast_to(chunk[:, here], (ROWS, LANES))
            first = found[0:ROWS, here]
            rest = found[FOLD * ROWS:(FOLD + 1) * ROWS, here]
            for n in range(1, parts_of):
                at = (n // FOLD * (FOLD + 1) + n % FOLD) * ROWS
                first = jnp.where(part == n, found[at:at + ROWS, here], first)
                if n % FOLD == 0:
                    at = at + FOLD * ROWS
                    rest = jnp.where(part >= n, found[at:at + ROWS, here], rest)
            rest = jnp.where(row8 // PAIR == part % FOLD, rest, 0.0)
            turn = PAIR
            while turn < ROWS:
                rest = rest + pltpu.roll(rest, turn, 0)
                turn *= 2
            second = jnp.where(row8 < TOP, pltpu.roll(first, ROWS - HARMS, 0), rest)
            for d in range(LANES // share):
                left = first if d == 0 else pltpu.roll(first, LANES - d * share, 1)
                move = (HALF - d * share) % LANES
                rest = second if move == 0 else pltpu.roll(second, move, 1)
                to = z * (LANES // share) + d
                part_buf[to % 2, to // 2, pl.ds(s, ROWS, stride=stations), :] = jnp.where(
                    lane8 < HALF, left, rest
                )

    groups = groups_of(stations)
    for g, group in enumerate(groups):
        for s in group:
            load(s).wait()
        if g == len(groups) - 1:
            @pl.when(jnp.logical_not(late))
            def _():
                open_up(range(evt_count - 1, 0, -1))


        before = list(groups[g - 1]) if g else []
        for n, s in enumerate(group):
            right_sides(s)
            if n < len(before):
                pick(before[n])
        for s in before[len(group):]:
            pick(s)
    for s in groups[-1]:
        pick(s)
    @pl.when(jnp.logical_not(is_first))
    def _():
        far(sta, evt).start()

    part_swap.start()

    block = tile_rows(tiles)
    rows = lax.broadcasted_iota(jnp.int32, (block, LANES), 0)
    columns = lax.broadcasted_iota(jnp.int32, (block, LANES), 1)
    tile_of_row = jnp.zeros((block, LANES), jnp.int32)
    for t in range(1, tiles + 1):
        tile_of_row = tile_of_row + jnp.where(rows >= t * HARMS, 1, 0)
    harm_of_row = rows - tile_of_row * HARMS
    within = columns
    for n in range(1, SPLITS):
        within = within - jnp.where(columns >= n * used, used, 0)
    harm_of_column = lax.shift_right_logical(within, 3)
    fits_in = jnp.logical_and(
        jnp.logical_and(harm_of_row == harm_of_column, columns < SPLITS * used),
        tile_of_row < tiles,
    )
    station_of_column = lax.bitwise_and(within, stations - 1)
    tile_of_column = jnp.zeros((block, LANES), jnp.int32)
    for s in range(stations):
        tile_of_column = jnp.where(
            station_of_column == s, tile_ref[sta * stations + s], tile_of_column
        )
    pieces = []
    for j in range(sta_count):
        here = jnp.logical_and(fits_in, tile_of_column == tile_of_row + j * tiles)
        pieces.append(jnp.where(here, 1.0, 0.0).astype(f32))
    choose = jnp.concatenate(pieces, axis=0).astype(jnp.bfloat16)

    pl.semaphore_wait(open_sem, sta_count - 1)
    for j in range(1, evt_count):
        normals(j).wait_recv()
    row = normal_buf[0:1] + jnp.sum(normal_recv[:, 0:1], axis=0)
    def factor(row):
        entries = jnp.broadcast_to(row, (stations, LANES))
        matrix = {}
        place = 0
        for k in range(HARMS):
            for l in range(k + 1):
                value = pick_lanes(entries, TERMS * station_ids + place)
                matrix[k, l] = value + 1.0 if k == l else value
                place += 1
        inverse = []
        ratio = {}
        for p in range(HARMS):
            inverse.append(1.0 / matrix[p, p])
            for k in range(p + 1, HARMS):
                ratio[k, p] = matrix[k, p] * inverse[p]
                for l in range(p + 1, k + 1):
                    matrix[k, l] = matrix[k, l] - ratio[k, p] * matrix[l, p]
        return inverse, ratio

    def solve(right, inverse, ratio):
        right = list(right)
        for p in range(HARMS):
            for k in range(p + 1, HARMS):
                right[k] = right[k] - ratio[k, p] * right[p]
        solved = [None] * HARMS
        for k in reversed(range(HARMS)):
            value = right[k] * inverse[k]
            for l in range(k + 1, HARMS):
                value = value - ratio[l, k] * solved[l]
            solved[k] = value
        layers = []
        for n in range(SPLITS):
            coarse = [value.astype(jnp.bfloat16).astype(f32) for value in solved]
            layers += coarse
            solved = [value - part for value, part in zip(solved, coarse)]
        layers += [jnp.zeros((stations, LANES), f32)] * (LANES // stations - len(layers))
        return jnp.concatenate(layers, axis=0).astype(jnp.bfloat16)

    normal_buf[1:2] = row
    inverse, ratio = factor(row)

    part_swap.wait_recv()
    stacked = []
    for z in range(chips):
        right = [
            part_buf[core, z, k * stations:(k + 1) * stations]
            + part_pair[z, k * stations:(k + 1) * stations]
            for k in range(HARMS)
        ]
        stacked.append(solve(right, inverse, ratio))
    summed = jnp.dot(
        choose, jnp.concatenate(stacked, axis=1), preferred_element_type=f32
    )
    for z in range(chips):
        for j in range(sta_count):
            tile_buf[z, j] = summed[j * block:(j + 1) * block, z * LANES:(z + 1) * LANES]

    def send(to_sta, to_chip):
        @pl.when(is_sent(to_sta, to_chip))
        def _():
            sums(to_sta, to_chip).start()

    peers(send)

    members = jnp.zeros((block, LANES), f32)
    for s in range(sta_count * stations):
        members = members + jnp.where(tile_of_row + sta * tiles == tile_ref[s], 1.0, 0.0)
    scale = 1.0 / jnp.maximum(members, 1.0)

    part_swap.wait_send()
    for j in range(1, evt_count):
        normals(j).wait_send()

    def sent_out(to_sta, to_chip):
        @pl.when(is_sent(to_sta, to_chip))
        def _():
            sums(to_sta, to_chip).wait_send()

    peers(sent_out)

    @pl.when(jnp.logical_not(is_first))
    def _():
        far(sta, evt).wait_send()

    @pl.when(sta != 0)
    def _():
        far_row(sta, evt).wait_send()

    @pl.when(is_first)
    def _():
        for j in range(1, sta_count):
            for n in range(evt_count):
                far_row(j, n).wait_recv()
        factors = [factor(normal_buf[1:2])]
        for j in range(1, sta_count):
            factors.append(factor(jnp.sum(far_normal[j, :, 0:1], axis=0)))
        chosen = []
        for j in range(sta_count):
            of = jnp.zeros((block, LANES), jnp.int32)
            for s in range(stations):
                of = jnp.where(station_of_column == s, tile_ref[j * stations + s], of)
            here = jnp.logical_and(fits_in, of == tile_of_row)
            chosen.append(jnp.where(here, 1.0, 0.0).astype(jnp.bfloat16))
        sides = [None] * sta_count
        for n in range(evt_count):
            for j in range(sta_count):
                if j or n:
                    far(j, n).wait_recv()
                    side = far_recv[j, n]
                else:
                    side = part_buf[0, 0, 0:used]
                sides[j] = side if n == 0 else sides[j] + side
        layers = [
            solve(
                [sides[j][k * stations:(k + 1) * stations] for k in range(HARMS)],
                *factors[j],
            )
            for j in range(sta_count)
        ]
        far_sum[...] = jnp.dot(
            jnp.concatenate(chosen, axis=1),
            jnp.concatenate(layers, axis=0),
            preferred_element_type=f32,
        )

    @pl.when(jnp.logical_not(is_first))
    def _():
        total = tile_buf[chip, sta, 0:sent]
        for a in range(chips):
            for b in range(sta_count):
                if a or b:
                    from_chip, from_sta = lax.rem(chip + a, chips), lax.rem(sta + b, sta_count)
                    sums_from(from_sta, from_chip).wait_recv()
                    total = total + tile_recv[from_chip, from_sta, 0:sent]
        far_sum[0:sent] = total

    total = far_sum[0:sent]
    total = total * scale[0:sent]
    for t in range(tiles):
        for k in range(HARMS):
            row = total[t * HARMS + k:t * HARMS + k + 1]
            out_ref[t, k, 0:1, :] = row[:, 0:share]
            out_ref[t, k, 1:2, :] = row[:, HALF:HALF + share]

def body(evt_count, sta_count, traces, baz_bin, inc_bin, counts, depth_index, tile_of):
    _, stations, slots, samples = traces.shape
    depths = depth_index.shape[1]
    share = depths // evt_count
    chips = evt_count // 2
    pieces = -(-3 * slots // LANES)
    tiles = tile_count(tile_of.shape[0]) // sta_count
    vmem = pl.BlockSpec(memory_space=pltpu.VMEM)
    anywhere = pl.BlockSpec(memory_space=pl.ANY)
    f32 = jnp.float32
    used = HARMS * stations
    return pl.pallas_call(
        functools.partial(kernel, evt_count, sta_count, tiles),
        out_shape=pltpu.VMEM((tiles, HARMS, 2, share), f32),
        in_specs=[anywhere] * 6,
        out_specs=vmem,
        scratch_shapes=[
            pltpu.VMEM((stations, 3, slots, samples), traces.dtype),
            pltpu.VMEM(baz_bin.shape, jnp.int32),
            pltpu.VMEM(inc_bin.shape, jnp.int32),
            pltpu.SMEM(counts.shape, jnp.int32),
            pltpu.VMEM(depth_index.shape, jnp.int32),
            pltpu.SMEM(tile_of.shape, jnp.int32),
            pltpu.VMEM((pieces, 2 * ROWS * stations, LANES), f32),
            pltpu.VMEM((stations, 4 * ROWS, pieces * LANES), jnp.bfloat16),
            pltpu.VMEM((ROWS, LANES), f32),
            pltpu.VMEM((evt_count - 1, ROWS, LANES), f32),
            pltpu.VMEM((stations, samples // LANES * 2 * HARMS, 2 * LANES), jnp.bfloat16),
            pltpu.VMEM((stations, LANES, depths), jnp.bfloat16),
            pltpu.VMEM((2, chips, ROWS * stations, LANES), f32),
            pltpu.VMEM((chips, used, LANES), f32),
            pltpu.VMEM((chips, sta_count, tile_rows(tiles), LANES), f32),
            pltpu.VMEM((chips, sta_count, tile_rows(tiles), LANES), f32),
            pltpu.VMEM((sta_count, evt_count, used, LANES), f32),
            pltpu.VMEM((sta_count, evt_count, ROWS, LANES), f32),
            pltpu.VMEM((tile_rows(tiles), LANES), f32),
            pltpu.SemaphoreType.DMA((stations,)),
            pltpu.SemaphoreType.DMA((5,)),
            pltpu.SemaphoreType.DMA((2,)),
            pltpu.SemaphoreType.DMA((evt_count - 1,)),
            pltpu.SemaphoreType.DMA((evt_count - 1,)),
            pltpu.SemaphoreType.DMA((chips, sta_count)),
            pltpu.SemaphoreType.DMA((chips, sta_count)),
            pltpu.SemaphoreType.REGULAR,
            pltpu.SemaphoreType.DMA((2,)),
            pltpu.SemaphoreType.DMA((sta_count, evt_count)),
            pltpu.SemaphoreType.DMA((sta_count, evt_count)),
        ],
        compiler_params=pltpu.CompilerParams(collective_id=0, has_side_effects=True),
    )(traces, baz_bin, inc_bin, counts, depth_index, tile_of)


def tile_rows(tiles):
    return -(-tiles * HARMS // ROWS) * ROWS


def tile_count(stations):
    return stations // 2


def solution(mesh):
    return jax.shard_map(
        functools.partial(body, mesh.shape["evt"], mesh.shape["sta"]),
        mesh=mesh,
        in_specs=(
            P(None, "sta", "evt", None),
            P("sta", "evt"),
            P("sta", "evt"),
            P("sta"),
            P("sta", None),
            P(),
        ),
        out_specs=P("sta", None, None, "evt"),
        check_vma=False,
    )
```

```python
import functools

import jax
import jax.numpy as jnp
from jax import lax
from jax.experimental import pallas as pl
from jax.experimental.pallas import tpu as pltpu
from jax.sharding import PartitionSpec as P

BAZ_BINS = 36
HARMS = 5
LANES = 128
ROWS = 8
TERMS = 16
HALF = LANES // 2
TOP = ROWS - HARMS
PAIR = HARMS - TOP
FOLD = ROWS // PAIR
GROUPS = (4, 4)
SPLITS = 2
MESH = pl.DeviceIdType.MESH


def pick_lanes(values, lanes):
    return jnp.take_along_axis(values, lanes, axis=1, mode="promise_in_bounds")


def positions(c, k):
    if c == 0:
        return [k]
    if k < TOP:
        return [HARMS + k]
    return [ROWS + PAIR * n + HARMS - 1 - k for n in range(ROWS // PAIR)]


def groups_of(stations):
    groups, at = [], 0
    while at < stations:
        size = min(GROUPS[len(groups)] if len(groups) < len(GROUPS) else 1, stations - at)
        groups.append(range(at, at + size))
        at += size
    return groups


def kernel(
    evt_count,
    sta_count,
    tiles,
    traces_ref,
    baz_hbm,
    inc_hbm,
    counts_hbm,
    depth_hbm,
    tile_hbm,
    out_ref,
    trace_buf,
    baz_ref,
    inc_ref,
    counts_ref,
    depth_ref,
    tile_ref,
    weight_buf,
    left_buf,
    normal_buf,
    normal_recv,
    split_buf,
    hot_buf,
    part_buf,
    part_pair,
    tile_buf,
    tile_recv,
    far_recv,
    far_normal,
    far_sum,
    load_sem,
    small_sem,
    pair_sem,
    normal_send_sem,
    normal_recv_sem,
    tile_send_sem,
    tile_recv_sem,
    open_sem,
    far_send_sem,
    far_recv_sem,
    far_normal_sem,
):
    stations, slots = baz_ref.shape
    samples = traces_ref.shape[3]
    depths = depth_ref.shape[1]
    share = depths // evt_count
    used = HARMS * stations
    sent = HARMS * tiles
    evt = lax.axis_index("evt")
    sta = lax.axis_index("sta")
    chips = evt_count // 2
    core = evt % 2
    chip = evt // 2
    partner = {"evt": evt + 1 - 2 * core}
    f32 = jnp.float32

    def load(s):
        return pltpu.make_async_copy(traces_ref.at[:, s], trace_buf.at[s], load_sem.at[s])

    def peers(act):
        def one(n, carry):
            to_chip, to_sta = n // sta_count, n % sta_count

            @pl.when(jnp.logical_or(to_chip != chip, to_sta != sta))
            def _():
                act(to_sta, to_chip)

            return carry

        lax.fori_loop(0, chips * sta_count, one, 0, unroll=chips * sta_count <= 16)

    barrier = pltpu.get_barrier_semaphore()
    for j in range(1, evt_count):
        pl.semaphore_signal(
            barrier, inc=1, device_id={"evt": lax.rem(evt + j, evt_count)},
            device_id_type=MESH,
        )
    for j in range(1, sta_count):
        pl.semaphore_signal(
            barrier, inc=1, device_id={"sta": lax.rem(sta + j, sta_count)},
            device_id_type=MESH,
        )

    is_first = jnp.logical_and(evt == 0, sta == 0)
    no_mate = jnp.logical_and(evt != 0, sta != 0)

    @pl.when(is_first)
    def _():
        for j in range(1, sta_count):
            for n in range(1, evt_count):
                pl.semaphore_signal(
                    barrier, inc=1, device_id={"sta": j, "evt": n}, device_id_type=MESH
                )

    small = [
        pltpu.make_async_copy(src, dst, small_sem.at[n])
        for n, (src, dst) in enumerate(
            [
                (baz_hbm, baz_ref),
                (inc_hbm, inc_ref),
                (counts_hbm, counts_ref),
                (depth_hbm, depth_ref),
                (tile_hbm, tile_ref),
            ]
        )
    ]
    for copy in small:
        copy.start()
    for s in range(stations):
        load(s).start()

    for copy in small:
        copy.wait()

    phi = (baz_ref[...].astype(f32) + 0.5) * (2.0 * jnp.pi / BAZ_BINS)
    tilt = (12.0 + 2.5 * (inc_ref[...].astype(f32) + 0.5)) * (jnp.pi / 180.0)
    cosine, sine = jnp.cos(phi), jnp.sin(phi)
    cos_tilt, sin_tilt = jnp.cos(tilt), jnp.sin(tilt)
    row_ids = lax.broadcasted_iota(jnp.int32, (stations, slots), 0)
    total = jnp.zeros((stations, slots), jnp.int32)
    for s in range(stations):
        total = jnp.where(row_ids == s, counts_ref[s], total)
    slot_ids = evt * slots + lax.broadcasted_iota(jnp.int32, (stations, slots), 1)
    live = jnp.where(slot_ids < total, 1.0, 0.0).astype(f32)
    harm = [
        jnp.ones_like(phi),
        cosine,
        sine,
        2.0 * cosine * cosine - 1.0,
        2.0 * sine * cosine,
    ]
    weighted = [h * live for h in harm]
    lane_ids = lax.broadcasted_iota(jnp.int32, (stations, LANES), 1)
    station_ids = lax.broadcasted_iota(jnp.int32, (stations, LANES), 0)
    packed = jnp.zeros((stations, LANES), f32)
    place = 0
    for k in range(HARMS):
        for l in range(k + 1):
            column = jnp.sum(weighted[k] * harm[l], axis=1, keepdims=True)
            packed = jnp.where(lane_ids % TERMS == place, column, packed)
            place += 1
    packed = jnp.where(lane_ids // TERMS == station_ids, packed, 0.0)
    normal_buf[0:1] = jnp.sum(packed, axis=0, keepdims=True)

    def normals(j):
        return pltpu.make_async_remote_copy(
            src_ref=normal_buf.at[0:1],
            dst_ref=normal_recv.at[j - 1, 0:1],
            send_sem=normal_send_sem.at[j - 1],
            recv_sem=normal_recv_sem.at[j - 1],
            device_id={"evt": lax.rem(evt + j, evt_count)},
            device_id_type=MESH,
        )

    part_swap = pltpu.make_async_remote_copy(
        src_ref=part_buf.at[1 - core, :, 0:used],
        dst_ref=part_pair,
        send_sem=pair_sem.at[0],
        recv_sem=pair_sem.at[1],
        device_id=partner,
        device_id_type=MESH,
    )

    def sums(to_sta, to_chip):
        return pltpu.make_async_remote_copy(
            src_ref=tile_buf.at[to_chip, to_sta, 0:sent],
            dst_ref=tile_recv.at[chip, sta, 0:sent],
            send_sem=tile_send_sem.at[to_chip, to_sta],
            recv_sem=tile_recv_sem.at[chip, sta],
            device_id={"sta": to_sta, "evt": 2 * to_chip + core},
            device_id_type=MESH,
        )

    def far(from_sta, from_evt):
        return pltpu.make_async_remote_copy(
            src_ref=part_buf.at[0, 0, 0:used],
            dst_ref=far_recv.at[from_sta, from_evt],
            send_sem=far_send_sem.at[0],
            recv_sem=far_recv_sem.at[from_sta, from_evt],
            device_id={"sta": 0, "evt": 0},
            device_id_type=MESH,
        )

    def far_row(from_sta, from_evt):
        return pltpu.make_async_remote_copy(
            src_ref=normal_buf.at[0:1],
            dst_ref=far_normal.at[from_sta, from_evt, 0:1],
            send_sem=far_send_sem.at[1],
            recv_sem=far_normal_sem.at[from_sta, from_evt],
            device_id={"sta": 0, "evt": 0},
            device_id_type=MESH,
        )

    def sums_from(from_sta, from_chip):
        return pltpu.make_async_remote_copy(
            src_ref=tile_buf.at[from_chip, from_sta, 0:sent],
            dst_ref=tile_recv.at[from_chip, from_sta, 0:sent],
            send_sem=tile_send_sem.at[from_chip, from_sta],
            recv_sem=tile_recv_sem.at[from_chip, from_sta],
            device_id={"sta": from_sta, "evt": 2 * from_chip + core},
            device_id_type=MESH,
        )

    late = 2 * chip >= chips

    def is_sent(to_sta, to_chip):
        return jnp.logical_or(to_sta != 0, jnp.logical_or(to_chip != 0, core != 0))

    def open_up(order):
        pl.semaphore_wait(barrier, evt_count - 1 + sta_count - 1 + jnp.where(no_mate, 1, 0))

        for j in order:
            normals(j).start()

        @pl.when(sta != 0)
        def _():
            far_row(sta, evt).start()

        for j in range(1, sta_count):
            pl.semaphore_signal(
                open_sem, inc=1, device_id={"sta": lax.rem(sta + j, sta_count)},
                device_id_type=MESH,
            )

    @pl.when(late)
    def _():
        open_up(range(1, evt_count))

    parts = [
        [sin_tilt, -cos_tilt * cosine, -cos_tilt * sine],
        [jnp.zeros_like(phi), sine, -cosine],
    ]
    for c in range(2):
        for k in range(HARMS):
            for m in range(3):
                lane = m * slots
                weight = weighted[k] * parts[c][m]
                for position in positions(c, k):
                    at = position * stations
                    weight_buf[
                        lane // LANES, at:at + stations, lane % LANES:lane % LANES + slots
                    ] = weight
    for s in range(stations):
        for n in range(weight_buf.shape[0]):
            weights = weight_buf[n, pl.ds(s, 2 * ROWS, stride=stations), :]
            high = weights.astype(jnp.bfloat16)
            low = (weights - high.astype(f32)).astype(jnp.bfloat16)
            left_buf[s, 0:2 * ROWS, n * LANES:(n + 1) * LANES] = high
            left_buf[s, 2 * ROWS:4 * ROWS, n * LANES:(n + 1) * LANES] = low

    lane8 = lax.broadcasted_iota(jnp.int32, (ROWS, LANES), 1)
    row8 = lax.broadcasted_iota(jnp.int32, (ROWS, LANES), 0)

    parts_of = samples // LANES
    window_ids = lax.broadcasted_iota(jnp.int32, (LANES, depths), 0)

    def right_sides(s):
        block = trace_buf[s].reshape(3 * slots, samples)
        right = jnp.dot(left_buf[s, :, 0:3 * slots], block, preferred_element_type=f32)
        pair = right[0:2 * ROWS] + right[2 * ROWS:4 * ROWS]
        pair = pair + pltpu.roll(pair, samples - 1, 1)
        blocks = []
        for q in range(0, parts_of, FOLD):
            rest = pair[ROWS:2 * ROWS, q * LANES:(q + 1) * LANES]
            for n in range(FOLD):
                part = pair[:, (q + n) * LANES:(q + n + 1) * LANES]
                blocks.append(part[0:ROWS])
                if n:
                    rest = jnp.where(row8 // PAIR == n, part[ROWS:2 * ROWS], rest)
            blocks.append(rest)
        stacked = jnp.concatenate(blocks, axis=0)
        high = stacked.astype(jnp.bfloat16)
        split_buf[s, :, 0:LANES] = high
        split_buf[s, :, LANES:] = (stacked - high.astype(f32)).astype(jnp.bfloat16)
        lane = lax.bitwise_and(depth_ref[s:s + 1, :], LANES - 1)
        hot = jnp.where(window_ids == lane, 0.5, 0.0).astype(jnp.bfloat16)
        hot_buf[s] = hot

    def pick(s):
        hot = hot_buf[s]
        found = jnp.dot(
            split_buf[s], jnp.concatenate([hot, hot], axis=0), preferred_element_type=f32
        )
        chunk = lax.shift_right_logical(depth_ref[s:s + 1, :], 7)
        for z in range(depths // LANES):
            here = slice(z * LANES, (z + 1) * LANES)
            part = jnp.broadcast_to(chunk[:, here], (ROWS, LANES))
            first = found[0:ROWS, here]
            rest = found[FOLD * ROWS:(FOLD + 1) * ROWS, here]
            for n in range(1, parts_of):
                at = (n // FOLD * (FOLD + 1) + n % FOLD) * ROWS
                first = jnp.where(part == n, found[at:at + ROWS, here], first)
                if n % FOLD == 0:
                    at = at + FOLD * ROWS
                    rest = jnp.where(part >= n, found[at:at + ROWS, here], rest)
            rest = jnp.where(row8 // PAIR == part % FOLD, rest, 0.0)
            turn = PAIR
            while turn < ROWS:
                rest = rest + pltpu.roll(rest, turn, 0)
                turn *= 2
            second = jnp.where(row8 < TOP, pltpu.roll(first, ROWS - HARMS, 0), rest)
            for d in range(LANES // share):
                left = first if d == 0 else pltpu.roll(first, LANES - d * share, 1)
                move = (HALF - d * share) % LANES
                rest = second if move == 0 else pltpu.roll(second, move, 1)
                to = z * (LANES // share) + d
                part_buf[to % 2, to // 2, pl.ds(s, ROWS, stride=stations), :] = jnp.where(
                    lane8 < HALF, left, rest
                )

    groups = groups_of(stations)
    for g, group in enumerate(groups):
        for s in group:
            load(s).wait()
        if g == len(groups) - 1:
            @pl.when(jnp.logical_not(late))
            def _():
                open_up(range(evt_count - 1, 0, -1))


        before = list(groups[g - 1]) if g else []
        for n, s in enumerate(group):
            right_sides(s)
            if n < len(before):
                pick(before[n])
        for s in before[len(group):]:
            pick(s)
    for s in groups[-1]:
        pick(s)
    @pl.when(jnp.logical_not(is_first))
    def _():
        far(sta, evt).start()

    part_swap.start()

    block = tile_rows(tiles)
    rows = lax.broadcasted_iota(jnp.int32, (block, LANES), 0)
    columns = lax.broadcasted_iota(jnp.int32, (block, LANES), 1)
    tile_of_row = jnp.zeros((block, LANES), jnp.int32)
    for t in range(1, tiles + 1):
        tile_of_row = tile_of_row + jnp.where(rows >= t * HARMS, 1, 0)
    harm_of_row = rows - tile_of_row * HARMS
    within = columns
    for n in range(1, SPLITS):
        within = within - jnp.where(columns >= n * used, used, 0)
    harm_of_column = lax.shift_right_logical(within, 3)
    fits_in = jnp.logical_and(
        jnp.logical_and(harm_of_row == harm_of_column, columns < SPLITS * used),
        tile_of_row < tiles,
    )
    station_of_column = lax.bitwise_and(within, stations - 1)
    tile_of_column = jnp.zeros((block, LANES), jnp.int32)
    for s in range(stations):
        tile_of_column = jnp.where(
            station_of_column == s, tile_ref[sta * stations + s], tile_of_column
        )
    pieces = []
    for j in range(sta_count):
        here = jnp.logical_and(fits_in, tile_of_column == tile_of_row + j * tiles)
        pieces.append(jnp.where(here, 1.0, 0.0).astype(f32))
    choose = jnp.concatenate(pieces, axis=0).astype(jnp.bfloat16)

    pl.semaphore_wait(open_sem, sta_count - 1)
    for j in range(1, evt_count):
        normals(j).wait_recv()
    row = normal_buf[0:1] + jnp.sum(normal_recv[:, 0:1], axis=0)
    def factor(row):
        entries = jnp.broadcast_to(row, (stations, LANES))
        matrix = {}
        place = 0
        for k in range(HARMS):
            for l in range(k + 1):
                value = pick_lanes(entries, TERMS * station_ids + place)
                matrix[k, l] = value + 1.0 if k == l else value
                place += 1
        inverse = []
        ratio = {}
        for p in range(HARMS):
            inverse.append(1.0 / matrix[p, p])
            for k in range(p + 1, HARMS):
                ratio[k, p] = matrix[k, p] * inverse[p]
                for l in range(p + 1, k + 1):
                    matrix[k, l] = matrix[k, l] - ratio[k, p] * matrix[l, p]
        return inverse, ratio

    def solve(right, inverse, ratio):
        right = list(right)
        for p in range(HARMS):
            for k in range(p + 1, HARMS):
                right[k] = right[k] - ratio[k, p] * right[p]
        solved = [None] * HARMS
        for k in reversed(range(HARMS)):
            value = right[k] * inverse[k]
            for l in range(k + 1, HARMS):
                value = value - ratio[l, k] * solved[l]
            solved[k] = value
        layers = []
        for n in range(SPLITS):
            coarse = [value.astype(jnp.bfloat16).astype(f32) for value in solved]
            layers += coarse
            solved = [value - part for value, part in zip(solved, coarse)]
        layers += [jnp.zeros((stations, LANES), f32)] * (LANES // stations - len(layers))
        return jnp.concatenate(layers, axis=0).astype(jnp.bfloat16)

    normal_buf[1:2] = row
    inverse, ratio = factor(row)

    part_swap.wait_recv()
    stacked = []
    for z in range(chips):
        right = [
            part_buf[core, z, k * stations:(k + 1) * stations]
            + part_pair[z, k * stations:(k + 1) * stations]
            for k in range(HARMS)
        ]
        stacked.append(solve(right, inverse, ratio))
    summed = jnp.dot(
        choose, jnp.concatenate(stacked, axis=1), preferred_element_type=f32
    )
    for z in range(chips):
        for j in range(sta_count):
            tile_buf[z, j] = summed[j * block:(j + 1) * block, z * LANES:(z + 1) * LANES]

    def send(to_sta, to_chip):
        @pl.when(is_sent(to_sta, to_chip))
        def _():
            sums(to_sta, to_chip).start()

    peers(send)

    members = jnp.zeros((block, LANES), f32)
    for s in range(sta_count * stations):
        members = members + jnp.where(tile_of_row + sta * tiles == tile_ref[s], 1.0, 0.0)
    scale = 1.0 / jnp.maximum(members, 1.0)

    part_swap.wait_send()
    for j in range(1, evt_count):
        normals(j).wait_send()

    def sent_out(to_sta, to_chip):
        @pl.when(is_sent(to_sta, to_chip))
        def _():
            sums(to_sta, to_chip).wait_send()

    peers(sent_out)

    @pl.when(jnp.logical_not(is_first))
    def _():
        far(sta, evt).wait_send()

    @pl.when(sta != 0)
    def _():
        far_row(sta, evt).wait_send()

    tile_recv[chip, sta] = tile_buf[chip, sta]
    @pl.when(is_first)
    def _():
        for j in range(1, sta_count):
            for n in range(evt_count):
                far_row(j, n).wait_recv()
        factors = [factor(normal_buf[1:2])]
        for j in range(1, sta_count):
            factors.append(factor(jnp.sum(far_normal[j, :, 0:1], axis=0)))
        chosen = []
        for j in range(sta_count):
            of = jnp.zeros((block, LANES), jnp.int32)
            for s in range(stations):
                of = jnp.where(station_of_column == s, tile_ref[j * stations + s], of)
            here = jnp.logical_and(fits_in, of == tile_of_row)
            chosen.append(jnp.where(here, 1.0, 0.0).astype(jnp.bfloat16))
        layers = []
        for j in range(sta_count):
            for n in range(evt_count):
                if j or n:
                    far(j, n).wait_recv()
            right = []
            for k in range(HARMS):
                at = slice(k * stations, (k + 1) * stations)
                terms = [far_recv[j, n, at] for n in range(evt_count) if j or n]
                if j == 0:
                    terms.append(part_buf[0, 0, at])
                right.append(functools.reduce(jnp.add, terms))
            layers.append(solve(right, *factors[j]))
        far_sum[...] = functools.reduce(
            jnp.add,
            [
                jnp.dot(left, right, preferred_element_type=f32)
                for left, right in zip(chosen, layers)
            ],
        )


    @pl.when(jnp.logical_not(is_first))
    def _():
        peers(lambda from_sta, from_chip: sums_from(from_sta, from_chip).wait_recv())
        far_sum[0:sent] = functools.reduce(
            jnp.add, [tile_recv[z, j, 0:sent] for z in range(chips) for j in range(sta_count)]
        )

    total = far_sum[0:sent]
    total = total * scale[0:sent]
    for t in range(tiles):
        for k in range(HARMS):
            row = total[t * HARMS + k:t * HARMS + k + 1]
            out_ref[t, k, 0:1, :] = row[:, 0:share]
            out_ref[t, k, 1:2, :] = row[:, HALF:HALF + share]

def body(evt_count, sta_count, traces, baz_bin, inc_bin, counts, depth_index, tile_of):
    _, stations, slots, samples = traces.shape
    depths = depth_index.shape[1]
    share = depths // evt_count
    chips = evt_count // 2
    pieces = -(-3 * slots // LANES)
    tiles = tile_count(tile_of.shape[0]) // sta_count
    vmem = pl.BlockSpec(memory_space=pltpu.VMEM)
    anywhere = pl.BlockSpec(memory_space=pl.ANY)
    f32 = jnp.float32
    used = HARMS * stations
    return pl.pallas_call(
        functools.partial(kernel, evt_count, sta_count, tiles),
        out_shape=pltpu.VMEM((tiles, HARMS, 2, share), f32),
        in_specs=[anywhere] * 6,
        out_specs=vmem,
        scratch_shapes=[
            pltpu.VMEM((stations, 3, slots, samples), traces.dtype),
            pltpu.VMEM(baz_bin.shape, jnp.int32),
            pltpu.VMEM(inc_bin.shape, jnp.int32),
            pltpu.SMEM(counts.shape, jnp.int32),
            pltpu.VMEM(depth_index.shape, jnp.int32),
            pltpu.SMEM(tile_of.shape, jnp.int32),
            pltpu.VMEM((pieces, 2 * ROWS * stations, LANES), f32),
            pltpu.VMEM((stations, 4 * ROWS, pieces * LANES), jnp.bfloat16),
            pltpu.VMEM((ROWS, LANES), f32),
            pltpu.VMEM((evt_count - 1, ROWS, LANES), f32),
            pltpu.VMEM((stations, samples // LANES * 2 * HARMS, 2 * LANES), jnp.bfloat16),
            pltpu.VMEM((stations, LANES, depths), jnp.bfloat16),
            pltpu.VMEM((2, chips, ROWS * stations, LANES), f32),
            pltpu.VMEM((chips, used, LANES), f32),
            pltpu.VMEM((chips, sta_count, tile_rows(tiles), LANES), f32),
            pltpu.VMEM((chips, sta_count, tile_rows(tiles), LANES), f32),
            pltpu.VMEM((sta_count, evt_count, used, LANES), f32),
            pltpu.VMEM((sta_count, evt_count, ROWS, LANES), f32),
            pltpu.VMEM((tile_rows(tiles), LANES), f32),
            pltpu.SemaphoreType.DMA((stations,)),
            pltpu.SemaphoreType.DMA((5,)),
            pltpu.SemaphoreType.DMA((2,)),
            pltpu.SemaphoreType.DMA((evt_count - 1,)),
            pltpu.SemaphoreType.DMA((evt_count - 1,)),
            pltpu.SemaphoreType.DMA((chips, sta_count)),
            pltpu.SemaphoreType.DMA((chips, sta_count)),
            pltpu.SemaphoreType.REGULAR,
            pltpu.SemaphoreType.DMA((2,)),
            pltpu.SemaphoreType.DMA((sta_count, evt_count)),
            pltpu.SemaphoreType.DMA((sta_count, evt_count)),
        ],
        compiler_params=pltpu.CompilerParams(collective_id=0, has_side_effects=True),
    )(traces, baz_bin, inc_bin, counts, depth_index, tile_of)


def tile_rows(tiles):
    return -(-tiles * HARMS // ROWS) * ROWS


def tile_count(stations):
    return stations // 2


def solution(mesh):
    return jax.shard_map(
        functools.partial(body, mesh.shape["evt"], mesh.shape["sta"]),
        mesh=mesh,
        in_specs=(
            P(None, "sta", "evt", None),
            P("sta", "evt"),
            P("sta", "evt"),
            P("sta"),
            P("sta", None),
            P(),
        ),
        out_specs=P("sta", None, None, "evt"),
        check_vma=False,
    )
```

```python
import functools

import jax
import jax.numpy as jnp
from jax import lax
from jax.experimental import pallas as pl
from jax.experimental.pallas import tpu as pltpu
from jax.sharding import PartitionSpec as P

BAZ_BINS = 36
HARMS = 5
LANES = 128
ROWS = 8
TERMS = 16
HALF = LANES // 2
TOP = ROWS - HARMS
PAIR = HARMS - TOP
FOLD = ROWS // PAIR
GROUPS = (4, 4)
SPLITS = 3
MESH = pl.DeviceIdType.MESH


def pick_lanes(values, lanes):
    return jnp.take_along_axis(values, lanes, axis=1, mode="promise_in_bounds")


def positions(c, k):
    if c == 0:
        return [k]
    if k < TOP:
        return [HARMS + k]
    return [ROWS + PAIR * n + HARMS - 1 - k for n in range(ROWS // PAIR)]


def groups_of(stations):
    groups, at = [], 0
    while at < stations:
        size = min(GROUPS[len(groups)] if len(groups) < len(GROUPS) else 1, stations - at)
        groups.append(range(at, at + size))
        at += size
    return groups


def kernel(
    evt_count,
    sta_count,
    tiles,
    traces_ref,
    baz_hbm,
    inc_hbm,
    counts_hbm,
    depth_hbm,
    tile_hbm,
    out_ref,
    trace_buf,
    baz_ref,
    inc_ref,
    counts_ref,
    depth_ref,
    tile_ref,
    weight_buf,
    left_buf,
    normal_buf,
    normal_recv,
    split_buf,
    hot_buf,
    part_buf,
    part_pair,
    tile_buf,
    tile_recv,
    far_recv,
    far_normal,
    far_sum,
    load_sem,
    small_sem,
    pair_sem,
    normal_send_sem,
    normal_recv_sem,
    tile_send_sem,
    tile_recv_sem,
    open_sem,
    far_send_sem,
    far_recv_sem,
    far_normal_sem,
):
    stations, slots = baz_ref.shape
    samples = traces_ref.shape[3]
    depths = depth_ref.shape[1]
    share = depths // evt_count
    used = HARMS * stations
    sent = HARMS * tiles
    evt = lax.axis_index("evt")
    sta = lax.axis_index("sta")
    chips = evt_count // 2
    core = evt % 2
    chip = evt // 2
    partner = {"evt": evt + 1 - 2 * core}
    f32 = jnp.float32

    def load(s):
        return pltpu.make_async_copy(traces_ref.at[:, s], trace_buf.at[s], load_sem.at[s])

    def peers(act):
        def one(n, carry):
            to_chip, to_sta = n // sta_count, n % sta_count

            @pl.when(jnp.logical_or(to_chip != chip, to_sta != sta))
            def _():
                act(to_sta, to_chip)

            return carry

        lax.fori_loop(0, chips * sta_count, one, 0, unroll=chips * sta_count <= 16)

    barrier = pltpu.get_barrier_semaphore()
    for j in range(1, evt_count):
        pl.semaphore_signal(
            barrier, inc=1, device_id={"evt": lax.rem(evt + j, evt_count)},
            device_id_type=MESH,
        )
    for j in range(1, sta_count):
        pl.semaphore_signal(
            barrier, inc=1, device_id={"sta": lax.rem(sta + j, sta_count)},
            device_id_type=MESH,
        )

    is_first = jnp.logical_and(evt == 0, sta == 0)
    no_mate = jnp.logical_and(evt != 0, sta != 0)

    @pl.when(is_first)
    def _():
        for j in range(1, sta_count):
            for n in range(1, evt_count):
                pl.semaphore_signal(
                    barrier, inc=1, device_id={"sta": j, "evt": n}, device_id_type=MESH
                )

    small = [
        pltpu.make_async_copy(src, dst, small_sem.at[n])
        for n, (src, dst) in enumerate(
            [
                (baz_hbm, baz_ref),
                (inc_hbm, inc_ref),
                (counts_hbm, counts_ref),
                (depth_hbm, depth_ref),
                (tile_hbm, tile_ref),
            ]
        )
    ]
    for copy in small:
        copy.start()
    for s in range(stations):
        load(s).start()

    for copy in small:
        copy.wait()

    phi = (baz_ref[...].astype(f32) + 0.5) * (2.0 * jnp.pi / BAZ_BINS)
    tilt = (12.0 + 2.5 * (inc_ref[...].astype(f32) + 0.5)) * (jnp.pi / 180.0)
    cosine, sine = jnp.cos(phi), jnp.sin(phi)
    cos_tilt, sin_tilt = jnp.cos(tilt), jnp.sin(tilt)
    row_ids = lax.broadcasted_iota(jnp.int32, (stations, slots), 0)
    total = jnp.zeros((stations, slots), jnp.int32)
    for s in range(stations):
        total = jnp.where(row_ids == s, counts_ref[s], total)
    slot_ids = evt * slots + lax.broadcasted_iota(jnp.int32, (stations, slots), 1)
    live = jnp.where(slot_ids < total, 1.0, 0.0).astype(f32)
    harm = [
        jnp.ones_like(phi),
        cosine,
        sine,
        2.0 * cosine * cosine - 1.0,
        2.0 * sine * cosine,
    ]
    weighted = [h * live for h in harm]
    lane_ids = lax.broadcasted_iota(jnp.int32, (stations, LANES), 1)
    station_ids = lax.broadcasted_iota(jnp.int32, (stations, LANES), 0)
    packed = jnp.zeros((stations, LANES), f32)
    place = 0
    for k in range(HARMS):
        for l in range(k + 1):
            column = jnp.sum(weighted[k] * harm[l], axis=1, keepdims=True)
            packed = jnp.where(lane_ids % TERMS == place, column, packed)
            place += 1
    packed = jnp.where(lane_ids // TERMS == station_ids, packed, 0.0)
    normal_buf[0:1] = jnp.sum(packed, axis=0, keepdims=True)

    def normals(j):
        return pltpu.make_async_remote_copy(
            src_ref=normal_buf.at[0:1],
            dst_ref=normal_recv.at[j - 1, 0:1],
            send_sem=normal_send_sem.at[j - 1],
            recv_sem=normal_recv_sem.at[j - 1],
            device_id={"evt": lax.rem(evt + j, evt_count)},
            device_id_type=MESH,
        )

    part_swap = pltpu.make_async_remote_copy(
        src_ref=part_buf.at[1 - core, :, 0:used],
        dst_ref=part_pair,
        send_sem=pair_sem.at[0],
        recv_sem=pair_sem.at[1],
        device_id=partner,
        device_id_type=MESH,
    )

    def sums(to_sta, to_chip):
        return pltpu.make_async_remote_copy(
            src_ref=tile_buf.at[to_chip, to_sta, 0:sent],
            dst_ref=tile_recv.at[chip, sta, 0:sent],
            send_sem=tile_send_sem.at[to_chip, to_sta],
            recv_sem=tile_recv_sem.at[chip, sta],
            device_id={"sta": to_sta, "evt": 2 * to_chip + core},
            device_id_type=MESH,
        )

    def far(from_sta, from_evt):
        return pltpu.make_async_remote_copy(
            src_ref=part_buf.at[0, 0, 0:used],
            dst_ref=far_recv.at[from_sta, from_evt],
            send_sem=far_send_sem.at[0],
            recv_sem=far_recv_sem.at[from_sta, from_evt],
            device_id={"sta": 0, "evt": 0},
            device_id_type=MESH,
        )

    def far_row(from_sta, from_evt):
        return pltpu.make_async_remote_copy(
            src_ref=normal_buf.at[0:1],
            dst_ref=far_normal.at[from_sta, from_evt, 0:1],
            send_sem=far_send_sem.at[1],
            recv_sem=far_normal_sem.at[from_sta, from_evt],
            device_id={"sta": 0, "evt": 0},
            device_id_type=MESH,
        )

    def sums_from(from_sta, from_chip):
        return pltpu.make_async_remote_copy(
            src_ref=tile_buf.at[from_chip, from_sta, 0:sent],
            dst_ref=tile_recv.at[from_chip, from_sta, 0:sent],
            send_sem=tile_send_sem.at[from_chip, from_sta],
            recv_sem=tile_recv_sem.at[from_chip, from_sta],
            device_id={"sta": from_sta, "evt": 2 * from_chip + core},
            device_id_type=MESH,
        )

    late = 2 * chip >= chips

    def is_sent(to_sta, to_chip):
        return jnp.logical_or(to_sta != 0, jnp.logical_or(to_chip != 0, core != 0))

    def open_up(order):
        pl.semaphore_wait(barrier, evt_count - 1 + sta_count - 1 + jnp.where(no_mate, 1, 0))

        @pl.when(sta != 0)
        def _():
            far_row(sta, evt).start()

        for j in order:
            normals(j).start()
        for j in range(1, sta_count):
            pl.semaphore_signal(
                open_sem, inc=1, device_id={"sta": lax.rem(sta + j, sta_count)},
                device_id_type=MESH,
            )

    @pl.when(late)
    def _():
        open_up([*range(2, evt_count), 1])

    parts = [
        [sin_tilt, -cos_tilt * cosine, -cos_tilt * sine],
        [jnp.zeros_like(phi), sine, -cosine],
    ]
    weight_buf[...] = jnp.zeros_like(weight_buf)
    for c in range(2):
        for k in range(HARMS):
            for m in range(3):
                lane = m * slots
                weight = weighted[k] * parts[c][m]
                for position in positions(c, k):
                    at = position * stations
                    weight_buf[
                        lane // LANES, at:at + stations, lane % LANES:lane % LANES + slots
                    ] = weight
    for s in range(stations):
        for n in range(weight_buf.shape[0]):
            weights = weight_buf[n, pl.ds(s, 2 * ROWS, stride=stations), :]
            high = weights.astype(jnp.bfloat16)
            low = (weights - high.astype(f32)).astype(jnp.bfloat16)
            left_buf[s, 0:2 * ROWS, n * LANES:(n + 1) * LANES] = high
            left_buf[s, 2 * ROWS:4 * ROWS, n * LANES:(n + 1) * LANES] = low

    lane8 = lax.broadcasted_iota(jnp.int32, (ROWS, LANES), 1)
    row8 = lax.broadcasted_iota(jnp.int32, (ROWS, LANES), 0)

    parts_of = samples // LANES
    window_ids = lax.broadcasted_iota(jnp.int32, (LANES, depths), 0)

    def right_sides(s):
        block = trace_buf[s].reshape(3 * slots, samples)
        right = jnp.dot(left_buf[s, :, 0:3 * slots], block, preferred_element_type=f32)
        pair = right[0:2 * ROWS] + right[2 * ROWS:4 * ROWS]
        pair = pair + pltpu.roll(pair, samples - 1, 1)
        blocks = []
        for q in range(0, parts_of, FOLD):
            rest = pair[ROWS:2 * ROWS, q * LANES:(q + 1) * LANES]
            for n in range(FOLD):
                part = pair[:, (q + n) * LANES:(q + n + 1) * LANES]
                blocks.append(part[0:ROWS])
                if n:
                    rest = jnp.where(row8 // PAIR == n, part[ROWS:2 * ROWS], rest)
            blocks.append(rest)
        stacked = jnp.concatenate(blocks, axis=0)
        high = stacked.astype(jnp.bfloat16)
        split_buf[s, :, 0:LANES] = high
        split_buf[s, :, LANES:] = (stacked - high.astype(f32)).astype(jnp.bfloat16)
        lane = lax.bitwise_and(depth_ref[s:s + 1, :], LANES - 1)
        hot = jnp.where(window_ids == lane, 0.5, 0.0).astype(jnp.bfloat16)
        hot_buf[s] = hot

    def pick(s):
        hot = hot_buf[s]
        found = jnp.dot(
            split_buf[s], jnp.concatenate([hot, hot], axis=0), preferred_element_type=f32
        )
        chunk = lax.shift_right_logical(depth_ref[s:s + 1, :], 7)
        for z in range(depths // LANES):
            here = slice(z * LANES, (z + 1) * LANES)
            part = jnp.broadcast_to(chunk[:, here], (ROWS, LANES))
            first = found[0:ROWS, here]
            rest = found[FOLD * ROWS:(FOLD + 1) * ROWS, here]
            for n in range(1, parts_of):
                at = (n // FOLD * (FOLD + 1) + n % FOLD) * ROWS
                first = jnp.where(part == n, found[at:at + ROWS, here], first)
                if n % FOLD == 0:
                    at = at + FOLD * ROWS
                    rest = jnp.where(part >= n, found[at:at + ROWS, here], rest)
            rest = jnp.where(row8 // PAIR == part % FOLD, rest, 0.0)
            turn = PAIR
            while turn < ROWS:
                rest = rest + pltpu.roll(rest, turn, 0)
                turn *= 2
            second = jnp.where(row8 < TOP, pltpu.roll(first, ROWS - HARMS, 0), rest)
            for d in range(LANES // share):
                left = first if d == 0 else pltpu.roll(first, LANES - d * share, 1)
                move = (HALF - d * share) % LANES
                rest = second if move == 0 else pltpu.roll(second, move, 1)
                to = z * (LANES // share) + d
                part_buf[to % 2, to // 2, pl.ds(s, ROWS, stride=stations), :] = jnp.where(
                    lane8 < HALF, left, rest
                )

    groups = groups_of(stations)
    for g, group in enumerate(groups):
        for s in group:
            load(s).wait()
        if g == len(groups) - 1:
            @pl.when(jnp.logical_not(late))
            def _():
                open_up(range(evt_count - 1, 0, -1))


        before = list(groups[g - 1]) if g else []
        for n, s in enumerate(group):
            right_sides(s)
            if n < len(before):
                pick(before[n])
        for s in before[len(group):]:
            pick(s)
    for s in groups[-1]:
        pick(s)
    @pl.when(jnp.logical_not(is_first))
    def _():
        far(sta, evt).start()

    part_swap.start()

    block = tile_rows(tiles)
    rows = lax.broadcasted_iota(jnp.int32, (block, LANES), 0)
    columns = lax.broadcasted_iota(jnp.int32, (block, LANES), 1)
    tile_of_row = jnp.zeros((block, LANES), jnp.int32)
    for t in range(1, tiles + 1):
        tile_of_row = tile_of_row + jnp.where(rows >= t * HARMS, 1, 0)
    harm_of_row = rows - tile_of_row * HARMS
    within = columns
    for n in range(1, SPLITS):
        within = within - jnp.where(columns >= n * used, used, 0)
    harm_of_column = lax.shift_right_logical(within, 3)
    fits_in = jnp.logical_and(
        jnp.logical_and(harm_of_row == harm_of_column, columns < SPLITS * used),
        tile_of_row < tiles,
    )
    station_of_column = lax.bitwise_and(within, stations - 1)
    tile_of_column = jnp.zeros((block, LANES), jnp.int32)
    for s in range(stations):
        tile_of_column = jnp.where(
            station_of_column == s, tile_ref[sta * stations + s], tile_of_column
        )
    pieces = []
    for j in range(sta_count):
        here = jnp.logical_and(fits_in, tile_of_column == tile_of_row + j * tiles)
        pieces.append(jnp.where(here, 1.0, 0.0).astype(f32))
    choose = jnp.concatenate(pieces, axis=0).astype(jnp.bfloat16)

    pl.semaphore_wait(open_sem, sta_count - 1)
    for j in range(1, evt_count):
        normals(j).wait_recv()
    row = normal_buf[0:1] + jnp.sum(normal_recv[:, 0:1], axis=0)
    def factor(row):
        entries = jnp.broadcast_to(row, (stations, LANES))
        matrix = {}
        place = 0
        for k in range(HARMS):
            for l in range(k + 1):
                value = pick_lanes(entries, TERMS * station_ids + place)
                matrix[k, l] = value + 1.0 if k == l else value
                place += 1
        inverse = []
        ratio = {}
        for p in range(HARMS):
            inverse.append(1.0 / matrix[p, p])
            for k in range(p + 1, HARMS):
                ratio[k, p] = matrix[k, p] * inverse[p]
                for l in range(p + 1, k + 1):
                    matrix[k, l] = matrix[k, l] - ratio[k, p] * matrix[l, p]
        return inverse, ratio

    def solve(right, inverse, ratio):
        right = list(right)
        for p in range(HARMS):
            for k in range(p + 1, HARMS):
                right[k] = right[k] - ratio[k, p] * right[p]
        solved = [None] * HARMS
        for k in reversed(range(HARMS)):
            value = right[k] * inverse[k]
            for l in range(k + 1, HARMS):
                value = value - ratio[l, k] * solved[l]
            solved[k] = value
        layers = []
        for n in range(SPLITS):
            coarse = [value.astype(jnp.bfloat16).astype(f32) for value in solved]
            layers += coarse
            solved = [value - part for value, part in zip(solved, coarse)]
        layers += [jnp.zeros((stations, LANES), f32)] * (LANES // stations - len(layers))
        return jnp.concatenate(layers, axis=0).astype(jnp.bfloat16)

    normal_buf[1:2] = row
    inverse, ratio = factor(row)

    part_swap.wait_recv()
    stacked = []
    for z in range(chips):
        right = [
            part_buf[core, z, k * stations:(k + 1) * stations]
            + part_pair[z, k * stations:(k + 1) * stations]
            for k in range(HARMS)
        ]
        stacked.append(solve(right, inverse, ratio))
    summed = jnp.dot(
        choose, jnp.concatenate(stacked, axis=1), preferred_element_type=f32
    )
    for z in range(chips):
        for j in range(sta_count):
            tile_buf[z, j] = summed[j * block:(j + 1) * block, z * LANES:(z + 1) * LANES]

    def send(to_sta, to_chip):
        @pl.when(is_sent(to_sta, to_chip))
        def _():
            sums(to_sta, to_chip).start()

    peers(send)

    members = jnp.zeros((block, LANES), f32)
    for s in range(sta_count * stations):
        members = members + jnp.where(tile_of_row + sta * tiles == tile_ref[s], 1.0, 0.0)
    scale = 1.0 / jnp.maximum(members, 1.0)

    part_swap.wait_send()
    for j in range(1, evt_count):
        normals(j).wait_send()

    def sent_out(to_sta, to_chip):
        @pl.when(is_sent(to_sta, to_chip))
        def _():
            sums(to_sta, to_chip).wait_send()

    peers(sent_out)

    @pl.when(jnp.logical_not(is_first))
    def _():
        far(sta, evt).wait_send()

    @pl.when(sta != 0)
    def _():
        far_row(sta, evt).wait_send()

    tile_recv[chip, sta] = tile_buf[chip, sta]
    @pl.when(is_first)
    def _():
        for j in range(1, sta_count):
            for n in range(evt_count):
                far_row(j, n).wait_recv()
        factors = [factor(normal_buf[1:2])]
        for j in range(1, sta_count):
            factors.append(factor(jnp.sum(far_normal[j, :, 0:1], axis=0)))
        chosen = []
        for j in range(sta_count):
            of = jnp.zeros((block, LANES), jnp.int32)
            for s in range(stations):
                of = jnp.where(station_of_column == s, tile_ref[j * stations + s], of)
            here = jnp.logical_and(fits_in, of == tile_of_row)
            chosen.append(jnp.where(here, 1.0, 0.0).astype(jnp.bfloat16))
        layers = []
        for j in range(sta_count):
            for n in range(evt_count):
                if j or n:
                    far(j, n).wait_recv()
            right = []
            for k in range(HARMS):
                at = slice(k * stations, (k + 1) * stations)
                terms = [far_recv[j, n, at] for n in range(evt_count) if j or n]
                if j == 0:
                    terms.append(part_buf[0, 0, at])
                right.append(functools.reduce(jnp.add, terms))
            layers.append(solve(right, *factors[j]))
        far_sum[...] = functools.reduce(
            jnp.add,
            [
                jnp.dot(left, right, preferred_element_type=f32)
                for left, right in zip(chosen, layers)
            ],
        )


    @pl.when(jnp.logical_not(is_first))
    def _():
        peers(lambda from_sta, from_chip: sums_from(from_sta, from_chip).wait_recv())
        far_sum[0:sent] = functools.reduce(
            jnp.add, [tile_recv[z, j, 0:sent] for z in range(chips) for j in range(sta_count)]
        )

    total = far_sum[0:sent]
    total = total * scale[0:sent]
    for t in range(tiles):
        for k in range(HARMS):
            row = total[t * HARMS + k:t * HARMS + k + 1]
            out_ref[t, k, 0:1, :] = row[:, 0:share]
            out_ref[t, k, 1:2, :] = row[:, HALF:HALF + share]

def body(evt_count, sta_count, traces, baz_bin, inc_bin, counts, depth_index, tile_of):
    _, stations, slots, samples = traces.shape
    depths = depth_index.shape[1]
    share = depths // evt_count
    chips = evt_count // 2
    pieces = -(-3 * slots // LANES)
    tiles = tile_count(tile_of.shape[0]) // sta_count
    vmem = pl.BlockSpec(memory_space=pltpu.VMEM)
    anywhere = pl.BlockSpec(memory_space=pl.ANY)
    f32 = jnp.float32
    used = HARMS * stations
    return pl.pallas_call(
        functools.partial(kernel, evt_count, sta_count, tiles),
        out_shape=pltpu.VMEM((tiles, HARMS, 2, share), f32),
        in_specs=[anywhere] * 6,
        out_specs=vmem,
        scratch_shapes=[
            pltpu.VMEM((stations, 3, slots, samples), traces.dtype),
            pltpu.VMEM(baz_bin.shape, jnp.int32),
            pltpu.VMEM(inc_bin.shape, jnp.int32),
            pltpu.SMEM(counts.shape, jnp.int32),
            pltpu.VMEM(depth_index.shape, jnp.int32),
            pltpu.SMEM(tile_of.shape, jnp.int32),
            pltpu.VMEM((pieces, 2 * ROWS * stations, LANES), f32),
            pltpu.VMEM((stations, 4 * ROWS, pieces * LANES), jnp.bfloat16),
            pltpu.VMEM((ROWS, LANES), f32),
            pltpu.VMEM((evt_count - 1, ROWS, LANES), f32),
            pltpu.VMEM((stations, samples // LANES * 2 * HARMS, 2 * LANES), jnp.bfloat16),
            pltpu.VMEM((stations, LANES, depths), jnp.bfloat16),
            pltpu.VMEM((2, chips, ROWS * stations, LANES), f32),
            pltpu.VMEM((chips, used, LANES), f32),
            pltpu.VMEM((chips, sta_count, tile_rows(tiles), LANES), f32),
            pltpu.VMEM((chips, sta_count, tile_rows(tiles), LANES), f32),
            pltpu.VMEM((sta_count, evt_count, used, LANES), f32),
            pltpu.VMEM((sta_count, evt_count, ROWS, LANES), f32),
            pltpu.VMEM((tile_rows(tiles), LANES), f32),
            pltpu.SemaphoreType.DMA((stations,)),
            pltpu.SemaphoreType.DMA((5,)),
            pltpu.SemaphoreType.DMA((2,)),
            pltpu.SemaphoreType.DMA((evt_count - 1,)),
            pltpu.SemaphoreType.DMA((evt_count - 1,)),
            pltpu.SemaphoreType.DMA((chips, sta_count)),
            pltpu.SemaphoreType.DMA((chips, sta_count)),
            pltpu.SemaphoreType.REGULAR,
            pltpu.SemaphoreType.DMA((2,)),
            pltpu.SemaphoreType.DMA((sta_count, evt_count)),
            pltpu.SemaphoreType.DMA((sta_count, evt_count)),
        ],
        compiler_params=pltpu.CompilerParams(collective_id=0, has_side_effects=True),
    )(traces, baz_bin, inc_bin, counts, depth_index, tile_of)


def tile_rows(tiles):
    return -(-tiles * HARMS // ROWS) * ROWS


def tile_count(stations):
    return stations // 2


def solution(mesh):
    return jax.shard_map(
        functools.partial(body, mesh.shape["evt"], mesh.shape["sta"]),
        mesh=mesh,
        in_specs=(
            P(None, "sta", "evt", None),
            P("sta", "evt"),
            P("sta", "evt"),
            P("sta"),
            P("sta", None),
            P(),
        ),
        out_specs=P("sta", None, None, "evt"),
        check_vma=False,
    )
```
